32 devices in a mesh: groups: 2 (over y), seq: 2 (over x), frame: 4 (over z), cfg: 2 (over core).
Axes of the slice: x: 2, y: 2, z: 4, core: 2. Of those that a mesh axis runs over, the one named last changes fastest.
Arguments:
- qkv: bfloat16 [2, 4096, 3, 4096], P('cfg', ('groups', 'frame', 'seq')), parts along dimension 1, may hold values from -108 to 108, as said below
- timestep: int32 [2], P('groups'), parts along dimension 0, may hold values from 0 to 999
- windows: int32 [32], replicated, may hold values from 0 to 2
- segments: int32 [16], P('groups'), parts along dimension 0, may hold values from 0 to 3, never falling along the last dimension, each value on 1 to 4 neighbouring positions
Outputs:
- guided: bfloat16 [4096, 16, 256], P(('groups', 'frame', 'seq'), 'cfg'), parts along dimension 0
The draws below stay inside these ranges and needn't reach their ends.
There are 2 independent parts, one for each index of `groups`. The reference program is written for one: setup_inputs(seed, part) draws one part's arguments, and reference() takes and returns one part's arrays. A program takes and returns all parts, laid end to end along the dimension named above; an argument that names none is the same for every part. Nothing has to cross between parts.
Inputs may be any that keep to these rules, and one draw needn't show every extreme that they name: Entries of qkv lie in this range. `segments`: shot numbers never fall from one frame to the next.
All inputs are finite; a program needn't handle non-finite values.
Results may differ from the reference program's by a relative error of at most 0.0053.
Values may be sent and summed in bfloat16 or wider, within the bound.
A program may use at most 128 MiB of HBM per device.

```python
import math
import jax
import jax.numpy as jnp
import numpy as np
from jax import lax

HD = 128
HEADS = 32
P_SIZE = 256
W_MAX = 2
SEGMENTS = 4
FRAMES = 8
TOKENS = 2048
N_SEQ = 2


def draw_qkv(key, part):
    key = jax.random.fold_in(key, 11)
    streams = jax.random.split(key, 1)
    shape = (2, TOKENS, 3, HEADS * HD)
    spreads = jnp.array([2.0, 1.0, 4.0], jnp.float32).reshape(1, 1, 3, 1)
    base = jnp.clip(jax.random.normal(streams[0], shape, jnp.float32), -5.0, 5.0)
    values = base * spreads
    return values.astype(jnp.bfloat16)


def draw_windows(key, part):
    key = jax.random.fold_in(key, 23)
    order = jax.random.permutation(key, HEADS)
    return (order % (W_MAX + 1)).astype(jnp.int32)


def length_profile(amount, total, most, slope):
    loads = [(1 << 20) // math.isqrt(rank ** slope) + 1 for rank in range(2, amount + 1)]
    spare, counts = total - most - (amount - 1), [1] * (amount - 1)
    while spare > 0:
        free = [i for i in range(amount - 1) if counts[i] < most]
        whole, left = sum([loads[i] for i in free]), spare
        for i in free:
            more = min(most - counts[i], max(1, left * loads[i] // whole), spare)
            counts[i] = counts[i] + more
            spare = spare - more
    return np.array([most] + counts)


def ragged(key, amount, total, most, slope):
    if amount == 2:
        one = jax.random.randint(key, (), max(1, total - most), min(most, total - 1) + 1)
        return jnp.stack([one, total - one])
    tallies = jnp.asarray(length_profile(amount, total, most, slope), jnp.int32)
    pairs = (amount - 1) // 2
    giver, taker = tallies[1:1 + 2 * pairs:2], tallies[2:2 + 2 * pairs:2]
    margin = jnp.minimum(giver - 1, most - taker)
    moved = jax.random.randint(jax.random.fold_in(key, 1), (pairs,), 0, 1 << 20) % (margin + 1)
    tallies = tallies.at[1:1 + 2 * pairs:2].set(giver - moved).at[2:2 + 2 * pairs:2].set(taker + moved)
    return tallies[jax.random.permutation(jax.random.fold_in(key, 2), amount)]


def setup_inputs(seed: int = 0, part: int = 0) -> dict:
    keys = jax.random.split(jax.random.key(seed), 5)
    own_keys = jax.random.split(jax.random.fold_in(keys[4], part), 5)
    qkv = draw_qkv(jax.random.fold_in(jax.random.fold_in(keys[4], part), 71), part)
    timestep = jax.random.randint(own_keys[1], (1,), 0, 1000).astype(jnp.int32)
    windows = draw_windows(jax.random.fold_in(keys[4], 71), part)
    segments = jnp.searchsorted(jnp.cumsum(ragged(own_keys[3], SEGMENTS, FRAMES, FRAMES // 2, 1)), jnp.arange(FRAMES), side="right").astype(jnp.int32)
    return {"qkv": qkv, "timestep": timestep, "windows": windows, "segments": segments}


def reference(qkv, timestep, windows, segments):
    scale = 1.0 / (HD ** 0.5)
    blocks = qkv.reshape(2, FRAMES, P_SIZE, 3, HEADS, HD)
    fill = jnp.full((W_MAX,), -1, jnp.int32)
    seg_pad = jnp.concatenate([fill, segments.astype(jnp.int32), fill])
    offsets = jnp.arange(2 * W_MAX + 1, dtype=jnp.int32) - W_MAX
    within_reach = jnp.abs(offsets)[None, :] <= windows.astype(jnp.int32)[:, None]

    def one_frame(frame_number):
        query = lax.dynamic_index_in_dim(blocks, frame_number, 1, keepdims=False)[:, :, 0]
        picks = jnp.clip(frame_number + offsets, 0, FRAMES - 1).astype(jnp.int32)
        near = jnp.take(blocks, picks, axis=1)
        key_rows = near[:, :, :, 1]
        value_rows = near[:, :, :, 2]
        shots = lax.dynamic_slice_in_dim(seg_pad, frame_number, 2 * W_MAX + 1, 0)
        own_shot = lax.dynamic_index_in_dim(seg_pad, frame_number + W_MAX, 0, keepdims=False)
        allowed = within_reach & (shots == own_shot)[None, :]
        scores = jnp.einsum('bthd,bgrhd->bhtgr', query.astype(jnp.float32), key_rows.astype(jnp.float32)) * scale
        scores = jnp.where(allowed[None, :, None, :, None], scores, -1e30)
        highest = jnp.max(scores, axis=(3, 4), keepdims=True)
        expd = jnp.exp(scores - highest)
        totals = jnp.sum(expd, axis=(3, 4))
        weights = expd.astype(jnp.bfloat16)
        mixed = jnp.einsum('bhtgr,bgrhd->bthd', weights.astype(jnp.float32), value_rows.astype(jnp.float32))
        mixed = mixed / jnp.transpose(totals, (0, 2, 1))[..., None]
        return mixed.astype(jnp.bfloat16)

    attended = lax.map(one_frame, jnp.arange(FRAMES, dtype=jnp.int32))
    strength = 1.0 + 4.0 * timestep[0].astype(jnp.float32) / 999.0
    cond = attended[:, 0].astype(jnp.float32)
    uncond = attended[:, 1].astype(jnp.float32)
    guided = (uncond + strength * (cond - uncond)).astype(jnp.bfloat16)
    guided = guided.reshape(TOKENS, N_SEQ, HEADS // N_SEQ, HD)
    guided = jnp.transpose(guided, (0, 2, 1, 3)).reshape(TOKENS, HEADS // N_SEQ, N_SEQ * HD)
    return guided
```

```python
import functools
import math

import jax
import jax.numpy as jnp
from jax import lax
from jax.experimental import pallas as pl
from jax.experimental.pallas import tpu as pltpu
from jax.sharding import PartitionSpec as P

HD = 128
W_MAX = 2
NEG = -1e30
LOG2E = 1.4426950408889634
MESH = pl.DeviceIdType.MESH
KV_EARLY = 2
KV_EVERY = 4


def gather_kernel(heads_all, levels, room, x_ref, win_ref, out_ref, fits_ref, sem):
    def copy(head, slot):
        return pltpu.make_async_copy(
            x_ref.at[:, :, pl.ds(pl.multiple_of(head * HD, HD), HD)], out_ref.at[slot], sem
        )

    def place(level):
        def step(head, slot):
            hit = win_ref[head] == level

            @pl.when(hit)
            def _():
                copy(head, slot).start()

            return slot + hit.astype(jnp.int32)

        return step

    slot = jnp.int32(0)
    fits = jnp.int32(1)
    for level in range(levels, -1, -1):
        slot = lax.fori_loop(0, heads_all, place(level), slot)
        if level:
            fits = fits * (slot <= room[level - 1]).astype(jnp.int32)
    fits_ref[0] = fits
    pltpu.make_async_copy(out_ref, out_ref, sem).wait()


def kernel(
    dims, x_ref, time_ref, win_ref, seg_ref, out_ref,
    kv, qb, gb, lb, every, rank_ref,
    kv_sem, q_sem, halo_sem, out_sem, a2a_send, own_send, relay_send, out_send, core_send,
    l_sem, l_send,
):
    S, C, F, heads, tl, frames_here, wide, near, short = dims
    groups = S * C
    rows = S * tl
    per_frame = rows // frames_here
    frames = F * frames_here
    s = lax.axis_index("seq")
    c = lax.axis_index("cfg")
    f = lax.axis_index("frame")
    partners = [(ds, dc) for ds in range(S) for dc in range(C) if ds or dc]
    others = [(i, ds, dc) for i, (ds, dc) in enumerate(partners) if ds]
    up_ok = f < F - 1
    down_ok = f > 0

    def at(ds, dc):
        return lax.rem(s + ds, S), lax.rem(c + dc, C)

    def rank(h, s2, c2):
        return h * groups + c2 * S + s2

    def token_rows(base, piece):
        return pl.ds(pl.multiple_of(base + piece * tl, tl), tl)

    def full(core):
        return wide - jnp.where(core > 0, short, 0)

    def shared(core):
        return near - jnp.where(core > 0, short, 0)

    low = near - short

    barrier = pltpu.get_barrier_semaphore()
    for ds, dc in partners:
        s2, c2 = at(ds, dc)
        pl.semaphore_signal(
            barrier, inc=1, device_id={"seq": s2, "cfg": c2}, device_id_type=MESH
        )
    for step in (-1, 1):
        @pl.when((f + step >= 0) & (f + step < F))
        def _():
            for dc in range(C):
                pl.semaphore_signal(
                    barrier, inc=1,
                    device_id={"frame": f + step, "cfg": lax.rem(c + dc, C)},
                    device_id_type=MESH,
                )
    beside = jnp.where(f > 0, C, 0) + jnp.where(f < F - 1, C, 0)
    pl.semaphore_wait(barrier, len(partners) + beside)

    def send_kv(i, ds, dc, h):
        s2, c2 = at(ds, dc)
        return pltpu.make_async_remote_copy(
            src_ref=x_ref.at[rank(h, s2, c2), pl.ds(1, 2)],
            dst_ref=kv.at[h, c, :, token_rows(rows, s), :],
            send_sem=a2a_send.at[0, h, i],
            recv_sem=kv_sem.at[h, s, c],
            device_id={"seq": s2, "cfg": c2}, device_id_type=MESH,
        )

    def send_q(i, ds, dc, h):
        s2, c2 = at(ds, dc)
        return pltpu.make_async_remote_copy(
            src_ref=x_ref.at[rank(h, s2, c2), 0],
            dst_ref=qb.at[h, c, token_rows(0, s), :],
            send_sem=a2a_send.at[1, h, i],
            recv_sem=q_sem.at[h, s, c],
            device_id={"seq": s2, "cfg": c2}, device_id_type=MESH,
        )

    def own_kv(h):
        return pltpu.make_async_copy(
            x_ref.at[rank(h, s, c), pl.ds(1, 2)],
            kv.at[h, c, :, token_rows(rows, s), :],
            kv_sem.at[h, s, c],
        )

    def own_q(h):
        return pltpu.make_async_copy(
            x_ref.at[rank(h, s, c), 0], qb.at[h, c, token_rows(0, s), :], q_sem.at[h, s, c]
        )

    def halo_base(side):
        return 0 if side == 0 else 2 * rows

    def neighbour(side):
        return f + (1 if side == 0 else -1)

    def send_halo(side, dc, h):
        c2 = lax.rem(c + dc, C)
        return pltpu.make_async_remote_copy(
            src_ref=x_ref.at[rank(h, s, c2), pl.ds(1, 2)],
            dst_ref=kv.at[h, c, :, token_rows(halo_base(side), s), :],
            send_sem=own_send.at[side, h, dc],
            recv_sem=halo_sem.at[side, h, s, c],
            device_id={"frame": neighbour(side), "cfg": c2}, device_id_type=MESH,
        )

    def relay(side, i, ds, dc, h):
        s2, b = at(ds, dc)
        return pltpu.make_async_remote_copy(
            src_ref=kv.at[h, b, :, token_rows(rows, s2), :],
            dst_ref=kv.at[h, b, :, token_rows(halo_base(side), s2), :],
            send_sem=relay_send.at[side, h, i],
            recv_sem=halo_sem.at[side, h, s2, b],
            device_id={"frame": neighbour(side)}, device_id_type=MESH,
        )

    def crosses(side, s2, h, core):
        return (h < full(core)) | (s2 == (S - 1 if side == 0 else 0))

    def send_out(ds, h):
        s2 = lax.rem(s + ds, S)
        return pltpu.make_async_remote_copy(
            src_ref=gb.at[h, token_rows(0, s2), :],
            dst_ref=every.at[rank(h, s, c)],
            send_sem=out_send.at[h, ds - 1],
            recv_sem=out_sem.at[rank(h, s, c)],
            device_id={"seq": s2}, device_id_type=MESH,
        )

    def send_core(h, s2, dc, src):
        return pltpu.make_async_remote_copy(
            src_ref=src,
            dst_ref=every.at[rank(h, s2, c)],
            send_sem=core_send.at[h, s2, dc - 1],
            recv_sem=out_sem.at[rank(h, s2, c)],
            device_id={"cfg": lax.rem(c + dc, C)}, device_id_type=MESH,
        )

    def send_local(h, s2, dc):
        c2 = lax.rem(c + dc, C)
        return pltpu.make_async_remote_copy(
            src_ref=x_ref.at[rank(h, s2, c2)],
            dst_ref=lb.at[h - low, s2, c],
            send_sem=l_send.at[h - low, s2, dc],
            recv_sem=l_sem.at[h - low, s2, c],
            device_id={"cfg": c2}, device_id_type=MESH,
        )

    def own_local(h, s2):
        return pltpu.make_async_copy(
            x_ref.at[rank(h, s2, c)], lb.at[h - low, s2, c], l_sem.at[h - low, s2, c]
        )

    def recv(ref, sem):
        pltpu.make_async_remote_copy(
            src_ref=ref, dst_ref=ref, send_sem=sem, recv_sem=sem,
            device_id={"seq": s}, device_id_type=MESH,
        ).wait_recv()

    sides = ((0, up_ok), (1, down_ok))

    def each_partner(h, act):
        for i, (ds, dc) in enumerate(partners):
            @pl.when(h < shared(lax.rem(c + dc, C)))
            def _():
                act(i, ds, dc, h)

    def each_halo(h, act):
        for side, ok in sides:
            for dc in range(C):
                c2 = lax.rem(c + dc, C)

                @pl.when(ok & (h < shared(c2)) & crosses(side, s, h, c2))
                def _():
                    act(send_halo(side, dc, h))

    def each_relay(i, ds, dc, h, act):
        s2, b = at(ds, dc)
        for side, ok in sides:
            @pl.when(ok & crosses(side, s2, h, c))
            def _():
                act(relay(side, i, ds, dc, h))

    def each_local(act):
        @pl.loop(low, heads)
        def _(h):
            for s2 in range(S):
                for dc in range(1, C):
                    @pl.when(h >= shared(lax.rem(c + dc, C)))
                    def _():
                        act(send_local(h, s2, dc))

    @pl.loop(0, near)
    def _(h):
        each_partner(h, lambda *k: send_kv(*k).start())
        each_halo(h, lambda copy: copy.start())

        @pl.when(h < shared(c))
        def _():
            own_kv(h).start()

    each_local(lambda copy: copy.start())

    @pl.loop(shared(c), heads)
    def _(h):
        for s2 in range(S):
            own_local(h, s2).start()

    @pl.loop(0, near)
    def _(h):
        each_partner(h, lambda *k: send_q(*k).start())

        @pl.when(h < shared(c))
        def _():
            own_q(h).start()

    for edge, base in ((f == 0, 0), (f == F - 1, 2 * rows)):
        @pl.when(edge)
        def _():
            @pl.loop(0, near)
            def _(h):
                kv[h, :, :, pl.ds(base, rows), :] = jnp.zeros((C, 2, rows, HD), kv.dtype)

    many = [jnp.int32(0)] * (W_MAX + 1)
    for head in range(heads * groups):
        for level in range(W_MAX + 1):
            many[level] = many[level] + jnp.where(win_ref[head] >= level, 1, 0)
    place = [many[level + 1] if level < W_MAX else jnp.int32(0) for level in range(W_MAX + 1)]
    for head in range(heads * groups):
        mine = place[0]
        for level in range(1, W_MAX + 1):
            mine = jnp.where(win_ref[head] == level, place[level], mine)
        rank_ref[head] = mine
        for level in range(W_MAX + 1):
            place[level] = place[level] + jnp.where(win_ref[head] == level, 1, 0)

    now = jnp.full((1, HD), time_ref[0], jnp.int32).astype(jnp.float32)
    strength = 1.0 + 4.0 * now / 999.0
    factor = LOG2E / math.sqrt(HD)

    def attend(query, keys, values, bias):
        scores = lax.dot_general(
            query, keys, (((1,), (1,)), ((), ())), preferred_element_type=jnp.float32
        )
        if bias is not None:
            scores = scores + bias
        top = jnp.max(scores, axis=1, keepdims=True)
        expd = jnp.exp2((scores - top) * factor)
        total = jnp.sum(expd, axis=1, keepdims=True)
        part = jnp.dot(expd.astype(jnp.bfloat16), values, preferred_element_type=jnp.float32)
        return (part / total).astype(jnp.bfloat16).astype(jnp.float32)

    def guide(cond, uncond):
        return (uncond + strength * (cond - uncond)).astype(jnp.bfloat16)

    @pl.loop(shared(c), heads)
    def _(h):
        for s2 in range(S):
            own_local(h, s2).wait()
            for dc in range(1, C):
                b = lax.rem(c + dc, C)
                recv(lb.at[h - low, s2, b], l_sem.at[h - low, s2, b])
            cond, uncond = [
                attend(lb[h - low, s2, b, 0], lb[h - low, s2, b, 1], lb[h - low, s2, b, 2], None)
                for b in range(C)
            ]
            every[rank(h, s2, c)] = guide(cond, uncond)
            for dc in range(1, C):
                send_core(h, s2, dc, every.at[rank(h, s2, c)]).start()

    @pl.loop(0, shared(c))
    def _(h):
        for i, ds, dc in others:
            s2, b = at(ds, dc)
            recv(kv.at[h, b, :, token_rows(rows, s2), :], kv_sem.at[h, s2, b])
            each_relay(i, ds, dc, h, lambda copy: copy.start())

    def hand_on(h):
        for ds in range(1, S):
            s2 = lax.rem(s + ds, S)
            ref = every.at[rank(h, s2, c)]
            recv(ref, out_sem.at[rank(h, s2, c)])
            for dc in range(1, C):
                send_core(h, s2, dc, ref).start()

    for lo, hi, reach in ((0, full(c), W_MAX), (full(c), shared(c), 1)):
        @pl.loop(lo, hi)
        def _(h):
            own_kv(h).wait()
            own_q(h).wait()
            for ds, dc in partners:
                s2, b = at(ds, dc)
                if not ds:
                    recv(kv.at[h, b, :, token_rows(rows, s2), :], kv_sem.at[h, s2, b])
                recv(qb.at[h, b, token_rows(0, s2), :], q_sem.at[h, s2, b])
            for side, ok in ((0, down_ok), (1, up_ok)):
                for ds in range(S):
                    s2 = lax.rem(s + ds, S)

                    @pl.when(ok & crosses(side, s2, h, c))
                    def _():
                        for b in range(C):
                            recv(
                                kv.at[h, b, :, token_rows(halo_base(side), s2), :],
                                halo_sem.at[side, h, s2, b],
                            )
            me = rank(h, s, c)
            window = jnp.int32(0)
            for level in range(1, W_MAX + 1):
                window = window + jnp.where(me < many[level], 1, 0)
            for number in range(frames_here):
                here = f * frames_here + number
                own_shot = seg_ref[here]
                pieces = []
                for offset in range(-reach, reach + 1):
                    there = here + offset
                    shot = seg_ref[jnp.clip(there, 0, frames - 1)]
                    allowed = (
                        (there >= 0) & (there < frames)
                        & (shot == own_shot) & (abs(offset) <= window)
                    )
                    pieces.append(
                        jnp.full((1, per_frame), jnp.where(allowed, 0.0, NEG), jnp.float32)
                    )
                bias = jnp.concatenate(pieces, axis=1)
                keys = pl.ds((frames_here + number - reach) * per_frame, len(pieces) * per_frame)
                mine = pl.ds(number * per_frame, per_frame)
                cond, uncond = [
                    attend(qb[h, b, mine, :], kv[h, b, 0, keys, :], kv[h, b, 1, keys, :], bias)
                    for b in range(C)
                ]
                gb[h, mine, :] = guide(cond, uncond)
            for ds in range(1, S):
                send_out(ds, h).start()
            for dc in range(1, C):
                send_core(h, s, dc, gb.at[h, token_rows(0, s), :]).start()
            every[me] = gb[h, token_rows(0, s), :]

            @pl.when(h > 0)
            def _():
                hand_on(h - 1)

    hand_on(shared(c) - 1)

    @pl.loop(0, near)
    def _(h):
        each_partner(h, lambda *k: send_kv(*k).wait_send())
        each_partner(h, lambda *k: send_q(*k).wait_send())
        each_halo(h, lambda copy: copy.wait_send())

    @pl.loop(0, shared(c))
    def _(h):
        for i, ds, dc in others:
            each_relay(i, ds, dc, h, lambda copy: copy.wait_send())

    each_local(lambda copy: copy.wait_send())

    @pl.loop(0, heads)
    def _(h):
        for s2 in range(S):
            for dc in range(1, C):
                r = rank(h, s2, lax.rem(c + dc, C))
                recv(every.at[r], out_sem.at[r])

    half = heads
    for s2 in range(S):
        for i in range(half):
            head = s2 * (C * half) + c * half + i
            out_ref[i, :, s2 * HD : (s2 + 1) * HD] = every[rank_ref[head]]

    @pl.loop(0, shared(c))
    def _(h):
        for ds in range(1, S):
            send_out(ds, h).wait_send()

    @pl.loop(0, heads)
    def _(h):
        for s2 in range(S):
            for dc in range(1, C):
                send_core(h, s2, dc, every.at[rank(h, s2, c)]).wait_send()


def plan_kernel(heads_all, levels, room, win_ref, plan_ref, fits_ref):
    def place(level):
        def step(head, slot):
            hit = win_ref[head] == level

            @pl.when(hit)
            def _():
                plan_ref[slot] = head
                plan_ref[heads_all + head] = slot

            return slot + hit.astype(jnp.int32)

        return step

    slot = jnp.int32(0)
    fits = jnp.int32(1)
    for level in range(levels, -1, -1):
        slot = lax.fori_loop(0, heads_all, place(level), slot)
        if level:
            plan_ref[2 * heads_all + level - 1] = slot
            fits = fits * (slot <= room[level - 1]).astype(jnp.int32)
    fits_ref[0] = fits


def fast_kernel(
    dims, x_ref, plan_ref, time_ref, seg_ref, out_ref,
    xq, xk, xv, qs, kw, qv, qr, tb, tr, ts, tsr, oh, ohr, hs, hr, ov, ovr, vs, ws, wr, gs, gr, every,
    la, lr,
    load_sem, q_send, q_recv, f_send, f_recv, t_send, t_recv, k_send, k_recv, s_send, s_recv,
    c_send, c_recv, w_send, w_recv, g_send, g_recv, h_send, h_recv, e_send, e_recv,
    l_send, l_recv,
):
    F, heads_all, W, M, tl = dims
    N = M - W
    L = heads_all - M
    s = lax.axis_index("seq")
    c = lax.axis_index("cfg")
    f = lax.axis_index("frame")
    frames = 2 * F
    dz = 1 - 2 * s
    up_ok, down_ok = f < F - 1, f > 0
    fwd, back = f + dz, f - dz
    fwd_ok = (fwd >= 0) & (fwd < F)
    back_ok = (back >= 0) & (back < F)
    lanes = [slice(128 * j, 128 * (j + 1)) for j in range(tl // 128)]
    k = len(lanes)

    own = (xq, xk, xv)
    for part, ref in enumerate(own):
        @pl.loop(0, heads_all)
        def _(h):
            pltpu.make_async_copy(
                x_ref.at[part, :, pl.ds(pl.multiple_of(h * HD, HD), HD)], ref.at[h],
                load_sem.at[part],
            ).start()

    def loaded(part):
        pltpu.make_async_copy(own[part], own[part], load_sem.at[part]).wait()

    barrier = pltpu.get_barrier_semaphore()
    for axis, other in (("seq", 1 - s), ("cfg", 1 - c)):
        pl.semaphore_signal(barrier, inc=1, device_id={axis: other}, device_id_type=MESH)
    for ok, step in ((up_ok, 1), (down_ok, -1)):
        @pl.when(ok)
        def _():
            pl.semaphore_signal(
                barrier, inc=1, device_id={"frame": f + step}, device_id_type=MESH
            )

    def remote(src, dst, send, arrive, where):
        return pltpu.make_async_remote_copy(
            src_ref=src, dst_ref=dst, send_sem=send, recv_sem=arrive,
            device_id=where, device_id_type=MESH,
        )

    across = {"seq": 1 - s}
    beside = {"cfg": 1 - c}

    def send_q(i):
        return remote(qs.at[i], qv.at[i], q_send.at[i], q_recv.at[i], across)

    def send_fwd(n):
        return remote(qv.at[W + n], qr.at[n], f_send.at[n], f_recv.at[n], {"frame": fwd})

    def send_third(n):
        return (
            remote(tb.at[n], tr.at[n], t_send.at[0, n], t_recv.at[0, n], {"frame": back}),
            remote(ts.at[n], tsr.at[n], t_send.at[1, n], t_recv.at[1, n], {"frame": back}),
        )

    def send_kv(side, i):
        start = 0 if side == 0 else 2 * tl
        return remote(
            kw.at[i, :, pl.ds(tl, tl), :], kw.at[i, :, pl.ds(start, tl), :],
            k_send.at[side, i], k_recv.at[side, i], {"frame": f + 1 if side == 0 else f - 1},
        )

    def send_stats(i):
        return remote(hs.at[i], hr.at[i], s_send.at[i], s_recv.at[i], across)

    def send_near_stats():
        part = pl.ds(W, N)
        return remote(hs.at[part], hr.at[part], s_send.at[W], s_recv.at[W], across)

    def send_part(i):
        return remote(ov.at[i], ovr.at[i], c_send.at[i], c_recv.at[i], beside)

    def send_weight(i):
        return remote(ws.at[i], wr.at[i], w_send.at[i], w_recv.at[i], across)

    def send_guided(i):
        return remote(gs.at[i], gr.at[i], g_send.at[i], g_recv.at[i], across)

    def send_home(i):
        return remote(oh.at[i], ohr.at[i], h_send.at[i], h_recv.at[i], beside)

    def send_final(i):
        return remote(every.at[i], every.at[i], e_send.at[i], e_recv.at[i], beside)

    def send_local(n):
        return remote(la.at[n], lr.at[n], l_send.at[n], l_recv.at[n], beside)

    def mine(i):
        return lax.rem(i, 2) == c

    factor = LOG2E / math.sqrt(HD)
    rows_id = lax.broadcasted_iota(jnp.int32, (128, 128), 0)
    lanes_id = lax.broadcasted_iota(jnp.int32, (128, 128), 1)
    eye = rows_id == lanes_id
    now = jnp.full((1, HD), time_ref[0], jnp.int32).astype(jnp.float32)
    strength = 1.0 + 4.0 * now / 999.0
    coef = jnp.where(c == 0, strength, 1.0 - strength)

    def to_row(column):
        return [
            jnp.sum(jnp.where(eye, column[part], 0.0), axis=0, keepdims=True) for part in lanes
        ]

    def to_column(row):
        return jnp.concatenate(
            [
                jnp.sum(jnp.where(eye, row[j : j + 1], 0.0), axis=1, keepdims=True)
                for j in range(k)
            ],
            axis=0,
        )

    def attend(query, keys, values, bias=None):
        scores = lax.dot_general(
            query, keys, (((1,), (1,)), ((), ())), preferred_element_type=jnp.float32
        )
        if bias is not None:
            scores = scores + bias
        top = jnp.max(scores, axis=1, keepdims=True)
        expd = jnp.exp2((scores - top) * factor)
        total = jnp.sum(expd, axis=1, keepdims=True)
        part = jnp.dot(expd.astype(jnp.bfloat16), values, preferred_element_type=jnp.float32)
        return part / total, top, total

    def keep_stats(ref, i, top, total):
        for j, row in enumerate(to_row(top) + to_row(total)):
            ref[i, j : j + 1, :] = row

    me = 2 * f + s
    visitor = 2 * f + 1 - s
    beyond = me + 2 * dz

    def shot(frame):
        return seg_ref[jnp.clip(frame, 0, frames - 1)]

    same_visit = shot(me) == shot(visitor)
    same_beyond = fwd_ok & (shot(visitor) == shot(beyond))
    same_low = down_ok & (shot(me) == shot(me - 2))
    same_high = up_ok & (shot(me) == shot(me + 2))

    def reach(level, i):
        return i < plan_ref[2 * heads_all + level - 1]

    def piece(allowed):
        return jnp.full((1, tl), jnp.where(allowed, 0.0, NEG), jnp.float32)

    loaded(0)

    @pl.loop(0, M)
    def _(i):
        qs[i] = xq[plan_ref[i]]

    pl.semaphore_wait(
        barrier, 2 + jnp.where(up_ok, 1, 0) + jnp.where(down_ok, 1, 0)
    )

    @pl.loop(W, M)
    def _(i):
        send_q(i).start()

    loaded(1)
    loaded(2)

    @pl.loop(0, W)
    def _(i):
        for part in range(2):
            kw[i, part, pl.ds(tl, tl), :] = own[1 + part][plan_ref[i]]

    def spread_kv(i):
        for side, ok in ((0, up_ok), (1, down_ok)):
            @pl.when(ok)
            def _():
                send_kv(side, i).start()

    EARLY = min(W, KV_EARLY)
    for i in range(EARLY):
        spread_kv(i)

    for ok, start in ((down_ok, 0), (up_ok, 2 * tl)):
        @pl.when(jnp.logical_not(ok))
        def _():
            @pl.loop(0, W)
            def _(i):
                kw[i, :, pl.ds(start, tl), :] = jnp.zeros((2, tl, HD), kw.dtype)

    @pl.when(jnp.logical_not(fwd_ok))
    def _():
        @pl.loop(0, N)
        def _(n):
            tr[n] = jnp.zeros((tl, HD), tr.dtype)
            tsr[n] = jnp.zeros((2 * k, 128), tsr.dtype)

    @pl.loop(W, M)
    def _(i):
        here = plan_ref[i]
        out, top, total = attend(qs[i], xk[here], xv[here])
        oh[i] = out
        keep_stats(hs, i, top, total)

    send_near_stats().start()

    @pl.loop(0, W)
    def _(i):
        send_q(i).start()

    LAG = 2

    @pl.loop(0, max(N + LAG, L))
    def _(n):
        @pl.when(n < N)
        def _():
            i = W + n
            send_q(i).wait_recv()

            @pl.when(fwd_ok)
            def _():
                send_fwd(n).start()

            here = plan_ref[i]
            out, top, total = attend(qv[i], xk[here], xv[here])
            ov[i] = out
            keep_stats(vs, i, top, total)

        @pl.when((n >= LAG) & (n < N + LAG) & back_ok)
        def _():
            m = n - LAG
            send_fwd(m).wait_recv()
            here = plan_ref[W + m]
            out, top, total = attend(qr[m], xk[here], xv[here])
            tb[m] = out.astype(jnp.bfloat16)
            keep_stats(ts, m, top, total)
            for copy in send_third(m):
                copy.start()

        late = EARLY + n // KV_EVERY

        @pl.when((lax.rem(n, KV_EVERY) == KV_EVERY - 1) & (late < W))
        def _():
            spread_kv(late)

        @pl.when(n < L)
        def _():
            here = plan_ref[M + n]
            out, _, _ = attend(xq[here], xk[here], xv[here])
            la[n] = out.astype(jnp.bfloat16)
            send_local(n).start()

    spread = min(W, EARLY + max(N + LAG, L) // KV_EVERY)

    @pl.loop(spread, W)
    def _(i):
        spread_kv(i)

    def weigh(i, home, parts):
        tops = [
            ref[at, 0:k, :] + jnp.full((1, 128), jnp.where(ok, 0.0, NEG), jnp.float32)
            for ref, at, ok in parts
        ]
        tops.append(home[i, 0:k, :])
        high = functools.reduce(jnp.maximum, tops)
        sums = [ref[at, k : 2 * k, :] for ref, at, _ in parts] + [home[i, k : 2 * k, :]]
        mass = [jnp.exp2((top - high) * factor) * total for top, total in zip(tops, sums)]
        whole = sum(mass)
        shares = [part / whole for part in mass]
        ws[i] = shares[-1]
        send_weight(i).start()
        return [to_column(share) * coef for share in shares[:-1]]

    def hand_over(i):
        @pl.when(jnp.logical_not(mine(i)))
        def _():
            send_part(i).start()

    def join(i):
        @pl.when(mine(i))
        def _():
            send_part(i).wait_recv()
            gs[i] = (ov[i] + ovr[i]).astype(jnp.bfloat16)
            send_guided(i).start()

    def weigh_home(i):
        send_weight(i).wait_recv()
        oh[i] = oh[i] * (to_column(wr[i]) * coef)

        @pl.when(jnp.logical_not(mine(i)))
        def _():
            send_home(i).start()

    def finish(i):
        @pl.when(mine(i))
        def _():
            send_home(i).wait_recv()
            send_guided(i).wait_recv()
            every[i] = (gr[i].astype(jnp.float32) + oh[i] + ohr[i]).astype(jnp.bfloat16)
            send_final(i).start()

    send_near_stats().wait_recv()

    @pl.loop(0, N)
    def _(n):
        i = W + n

        @pl.when(fwd_ok)
        def _():
            for copy in send_third(n):
                copy.wait_recv()

        near = reach(1, i)
        first, second = weigh(
            i, hr, [(vs, i, near & same_visit), (tsr, n, near & same_beyond)]
        )
        ov[i] = first * ov[i] + second * tr[n].astype(jnp.float32)
        hand_over(i)

    @pl.loop(0, L)
    def _(n):
        send_local(n).wait_recv()
        here, there = la[n].astype(jnp.float32), lr[n].astype(jnp.float32)
        cond = jnp.where(c == 0, here, there)
        uncond = jnp.where(c == 0, there, here)
        every[M + n] = (uncond + strength * (cond - uncond)).astype(jnp.bfloat16)

    first_keys = pl.multiple_of(tl * (1 - s), tl)
    per = -(-N // W)

    @pl.loop(0, W + 4)
    def _(j):
        @pl.when(j < W)
        def _():
            send_q(j).wait_recv()

            @pl.when(down_ok)
            def _():
                send_kv(0, j).wait_recv()

            @pl.when(up_ok)
            def _():
                send_kv(1, j).wait_recv()

            wide = reach(2, j)
            near = reach(1, j)
            bias = jnp.concatenate(
                [piece(wide & same_low), piece(True), piece(wide & same_high)], axis=1
            )
            out, top, total = attend(qs[j], kw[j, 0], kw[j, 1], bias)
            oh[j] = out
            keep_stats(hs, j, top, total)
            send_stats(j).start()
            one = near & same_visit
            two = near & same_beyond
            bias = jnp.concatenate(
                [
                    piece(jnp.where(s == 0, one, two)),
                    piece(jnp.where(s == 0, two, one)),
                ],
                axis=1,
            )
            keys = pl.ds(first_keys, 2 * tl)
            out, top, total = attend(qv[j], kw[j, 0, keys, :], kw[j, 1, keys, :], bias)
            ov[j] = out
            keep_stats(vs, j, top, total)

        @pl.when((j >= 2) & (j < W + 2))
        def _():
            m = j - 2
            send_stats(m).wait_recv()
            (share,) = weigh(m, hr, [(vs, m, reach(1, m) & (same_visit | same_beyond))])
            ov[m] = share * ov[m]
            hand_over(m)

        for part in range(per):
            n = per * j + part

            @pl.when(n < N)
            def _():
                join(W + n)

            late = per * (j - 3) + part

            @pl.when((late >= 0) & (late < N))
            def _():
                weigh_home(W + late)

        @pl.when((j >= 2) & (j < W + 2))
        def _():
            join(j - 2)

        @pl.when(j >= 4)
        def _():
            weigh_home(j - 4)

        for part in range(per):
            late = per * (j - 3) + part

            @pl.when((late >= 0) & (late < N))
            def _():
                finish(W + late)

        @pl.when(j >= 4)
        def _():
            finish(j - 4)

    @pl.loop(0, M)
    def _(i):
        @pl.when(jnp.logical_not(mine(i)))
        def _():
            send_final(i).wait_recv()

    half = heads_all // 4
    for s2 in range(2):
        for i in range(half):
            head = s2 * (2 * half) + c * half + i
            out_ref[i, :, s2 * HD : (s2 + 1) * HD] = every[plan_ref[heads_all + head]]

    @pl.loop(0, M)
    def _(i):
        send_q(i).wait_send()
        send_weight(i).wait_send()

        @pl.when(mine(i))
        def _():
            send_guided(i).wait_send()
            send_final(i).wait_send()

        @pl.when(jnp.logical_not(mine(i)))
        def _():
            send_part(i).wait_send()
            send_home(i).wait_send()

    @pl.loop(0, N)
    def _(n):
        @pl.when(fwd_ok)
        def _():
            send_fwd(n).wait_send()

        @pl.when(back_ok)
        def _():
            for copy in send_third(n):
                copy.wait_send()

    send_near_stats().wait_send()

    @pl.loop(0, W)
    def _(i):
        send_stats(i).wait_send()
        for side, ok in ((0, up_ok), (1, down_ok)):
            @pl.when(ok)
            def _():
                send_kv(side, i).wait_send()

    @pl.loop(0, L)
    def _(n):
        send_local(n).wait_send()


def fast_call(F, heads_all, W, M, tl, number):
    N, L, k = M - W, heads_all - M, tl // 128
    dma = pltpu.SemaphoreType.DMA

    def block(count, dtype=jnp.bfloat16):
        return pltpu.VMEM((count, tl, HD), dtype)

    def small(count, rows):
        return pltpu.VMEM((count, rows, 128), jnp.float32)

    f32 = jnp.float32
    return pl.pallas_call(
        functools.partial(fast_kernel, (F, heads_all, W, M, tl)),
        out_shape=jax.ShapeDtypeStruct((heads_all // 4, tl, 2 * HD), jnp.bfloat16),
        in_specs=[pl.BlockSpec(memory_space=pl.ANY)]
        + [pl.BlockSpec(memory_space=pltpu.SMEM)] * 3,
        out_specs=pl.BlockSpec(memory_space=pltpu.VMEM),
        scratch_shapes=[
            block(heads_all), block(heads_all), block(heads_all),
            block(M), pltpu.VMEM((W, 2, 3 * tl, HD), jnp.bfloat16), block(M),
            block(N), block(N), block(N), small(N, 2 * k), small(N, 2 * k),
            block(M, f32), block(M, f32), small(M, 2 * k), small(M, 2 * k),
            block(M, f32), block(M, f32), small(M, 2 * k), small(M, k), small(M, k),
            block(M), block(M), block(heads_all), block(L), block(L),
            dma((3,)), dma((M,)), dma((M,)), dma((N,)), dma((N,)), dma((2, N)), dma((2, N)),
            dma((2, W)), dma((2, W)), dma((W + 1,)), dma((W + 1,)),
            dma((M,)), dma((M,)), dma((M,)), dma((M,)), dma((M,)), dma((M,)),
            dma((M,)), dma((M,)), dma((M,)), dma((M,)), dma((L,)), dma((L,)),
        ],
        compiler_params=pltpu.CompilerParams(
            collective_id=number, has_side_effects=True, vmem_limit_bytes=56 * 2**20
        ),
        name=f"visiting_attention_{number}",
    )


def body(qkv, timestep, windows, segments):
    S, C, F = (lax.axis_size(axis) for axis in ("seq", "cfg", "frame"))
    x = jnp.transpose(qkv[0], (1, 0, 2))
    tl = x.shape[1]
    heads = x.shape[2] // HD // (S * C)
    frames_here = segments.shape[0] // F
    assert frames_here == W_MAX and heads * S * C * HD == x.shape[2]
    rows = S * tl
    groups = S * C
    n = groups - 1
    dma = pltpu.SemaphoreType.DMA
    heads_all = heads * groups

    def general(x, timestep, windows, segments):
        ordered, _ = pl.pallas_call(
            functools.partial(gather_kernel, heads_all, W_MAX, (heads_all,) * W_MAX),
            out_shape=(
                jax.ShapeDtypeStruct((heads_all, 3, tl, HD), x.dtype),
                jax.ShapeDtypeStruct((1,), jnp.int32),
            ),
            in_specs=[pl.BlockSpec(memory_space=pl.ANY), pl.BlockSpec(memory_space=pltpu.SMEM)],
            out_specs=(
                pl.BlockSpec(memory_space=pltpu.VMEM),
                pl.BlockSpec(memory_space=pltpu.SMEM),
            ),
            scratch_shapes=[dma],
            name="order_heads",
            compiler_params=pltpu.CompilerParams(vmem_limit_bytes=56 * 2**20),
        )(x, windows)
        kept, near = 1, heads
        return pl.pallas_call(
            functools.partial(kernel, (S, C, F, heads, tl, frames_here, heads, heads, 0)),
            out_shape=jax.ShapeDtypeStruct((heads, tl, S * HD), jnp.bfloat16),
            in_specs=[pl.BlockSpec(memory_space=pl.ANY)]
            + [pl.BlockSpec(memory_space=pltpu.SMEM)] * 3,
            out_specs=pl.BlockSpec(memory_space=pltpu.VMEM),
            scratch_shapes=[
                pltpu.VMEM((near, C, 2, 3 * rows, HD), jnp.bfloat16),
                pltpu.VMEM((near, C, rows, HD), jnp.bfloat16),
                pltpu.VMEM((near, rows, HD), jnp.bfloat16),
                pltpu.VMEM((kept, S, C, 3, tl, HD), jnp.bfloat16),
                pltpu.VMEM((heads_all, tl, HD), jnp.bfloat16),
                pltpu.SMEM((heads_all,), jnp.int32),
                dma((near, S, C)),
                dma((near, S, C)),
                dma((2, near, S, C)),
                dma((heads_all,)),
                dma((2, near, n)),
                dma((2, near, C)),
                dma((2, near, n)),
                dma((near, max(S - 1, 1))),
                dma((heads, S, C - 1)),
                dma((kept, S, C)),
                dma((kept, S, C)),
            ],
            compiler_params=pltpu.CompilerParams(
                collective_id=0, has_side_effects=True, vmem_limit_bytes=40 * 2**20
            ),
            name="guided_attention_0",
        )(ordered, timestep, windows, segments)

    if S == C == frames_here == 2 and tl % 128 == 0 and heads_all >= 8:
        wide, near = heads_all // 3, 2 * heads_all // 3
        plan, fits = pl.pallas_call(
            functools.partial(plan_kernel, heads_all, W_MAX, (near, wide)),
            out_shape=(
                jax.ShapeDtypeStruct((2 * heads_all + W_MAX,), jnp.int32),
                jax.ShapeDtypeStruct((1,), jnp.int32),
            ),
            in_specs=[pl.BlockSpec(memory_space=pltpu.SMEM)],
            out_specs=(pl.BlockSpec(memory_space=pltpu.SMEM),) * 2,
            name="plan_heads",
        )(windows)

        def fast(x, plan, timestep, windows, segments):
            return fast_call(F, heads_all, wide, near, tl, 1)(x, plan, timestep, segments)

        def slow(x, plan, timestep, windows, segments):
            return general(x, timestep, windows, segments)

        out = lax.cond(fits[0] > 0, fast, slow, x, plan, timestep, windows, segments)
    else:
        out = general(x, timestep, windows, segments)
    return jnp.transpose(out, (1, 0, 2))


def solution(mesh):
    return jax.shard_map(
        body,
        mesh=mesh,
        in_specs=(P("cfg", ("groups", "frame", "seq"), None, None), P("groups"), P(), P("groups")),
        out_specs=P(("groups", "frame", "seq"), "cfg", None),
        check_vma=False,
    )
```

```python
import functools
import math

import jax
import jax.numpy as jnp
from jax import lax
from jax.experimental import pallas as pl
from jax.experimental.pallas import tpu as pltpu
from jax.sharding import PartitionSpec as P

HD = 128
W_MAX = 2
NEG = -1e30
LOG2E = 1.4426950408889634
MESH = pl.DeviceIdType.MESH
DZ_EARLY, BACK_EARLY = 1, 2
HOST_LAG, JOIN_LAG, HOME_LAG, DONE_LAG = 2, 3, 5, 6
NEAR_HOME_LAG, NEAR_DONE_LAG = 2, 3


def gather_kernel(heads_all, levels, room, x_ref, win_ref, out_ref, fits_ref, sem):
    def copy(head, slot):
        return pltpu.make_async_copy(
            x_ref.at[:, :, pl.ds(pl.multiple_of(head * HD, HD), HD)], out_ref.at[slot], sem
        )

    def place(level):
        def step(head, slot):
            hit = win_ref[head] == level

            @pl.when(hit)
            def _():
                copy(head, slot).start()

            return slot + hit.astype(jnp.int32)

        return step

    slot = jnp.int32(0)
    fits = jnp.int32(1)
    for level in range(levels, -1, -1):
        slot = lax.fori_loop(0, heads_all, place(level), slot)
        if level:
            fits = fits * (slot <= room[level - 1]).astype(jnp.int32)
    fits_ref[0] = fits
    pltpu.make_async_copy(out_ref, out_ref, sem).wait()


def kernel(
    dims, x_ref, time_ref, win_ref, seg_ref, out_ref,
    kv, qb, gb, lb, every, rank_ref,
    kv_sem, q_sem, halo_sem, out_sem, a2a_send, own_send, relay_send, out_send, core_send,
    l_sem, l_send,
):
    S, C, F, heads, tl, frames_here, wide, near, short = dims
    groups = S * C
    rows = S * tl
    per_frame = rows // frames_here
    frames = F * frames_here
    s = lax.axis_index("seq")
    c = lax.axis_index("cfg")
    f = lax.axis_index("frame")
    partners = [(ds, dc) for ds in range(S) for dc in range(C) if ds or dc]
    others = [(i, ds, dc) for i, (ds, dc) in enumerate(partners) if ds]
    up_ok = f < F - 1
    down_ok = f > 0

    def at(ds, dc):
        return lax.rem(s + ds, S), lax.rem(c + dc, C)

    def rank(h, s2, c2):
        return h * groups + c2 * S + s2

    def token_rows(base, piece):
        return pl.ds(pl.multiple_of(base + piece * tl, tl), tl)

    def full(core):
        return wide - jnp.where(core > 0, short, 0)

    def shared(core):
        return near - jnp.where(core > 0, short, 0)

    low = near - short

    barrier = pltpu.get_barrier_semaphore()
    for ds, dc in partners:
        s2, c2 = at(ds, dc)
        pl.semaphore_signal(
            barrier, inc=1, device_id={"seq": s2, "cfg": c2}, device_id_type=MESH
        )
    for step in (-1, 1):
        @pl.when((f + step >= 0) & (f + step < F))
        def _():
            for dc in range(C):
                pl.semaphore_signal(
                    barrier, inc=1,
                    device_id={"frame": f + step, "cfg": lax.rem(c + dc, C)},
                    device_id_type=MESH,
                )
    beside = jnp.where(f > 0, C, 0) + jnp.where(f < F - 1, C, 0)
    pl.semaphore_wait(barrier, len(partners) + beside)

    def send_kv(i, ds, dc, h):
        s2, c2 = at(ds, dc)
        return pltpu.make_async_remote_copy(
            src_ref=x_ref.at[rank(h, s2, c2), pl.ds(1, 2)],
            dst_ref=kv.at[h, c, :, token_rows(rows, s), :],
            send_sem=a2a_send.at[0, h, i],
            recv_sem=kv_sem.at[h, s, c],
            device_id={"seq": s2, "cfg": c2}, device_id_type=MESH,
        )

    def send_q(i, ds, dc, h):
        s2, c2 = at(ds, dc)
        return pltpu.make_async_remote_copy(
            src_ref=x_ref.at[rank(h, s2, c2), 0],
            dst_ref=qb.at[h, c, token_rows(0, s), :],
            send_sem=a2a_send.at[1, h, i],
            recv_sem=q_sem.at[h, s, c],
            device_id={"seq": s2, "cfg": c2}, device_id_type=MESH,
        )

    def own_kv(h):
        return pltpu.make_async_copy(
            x_ref.at[rank(h, s, c), pl.ds(1, 2)],
            kv.at[h, c, :, token_rows(rows, s), :],
            kv_sem.at[h, s, c],
        )

    def own_q(h):
        return pltpu.make_async_copy(
            x_ref.at[rank(h, s, c), 0], qb.at[h, c, token_rows(0, s), :], q_sem.at[h, s, c]
        )

    def halo_base(side):
        return 0 if side == 0 else 2 * rows

    def neighbour(side):
        return f + (1 if side == 0 else -1)

    def send_halo(side, dc, h):
        c2 = lax.rem(c + dc, C)
        return pltpu.make_async_remote_copy(
            src_ref=x_ref.at[rank(h, s, c2), pl.ds(1, 2)],
            dst_ref=kv.at[h, c, :, token_rows(halo_base(side), s), :],
            send_sem=own_send.at[side, h, dc],
            recv_sem=halo_sem.at[side, h, s, c],
            device_id={"frame": neighbour(side), "cfg": c2}, device_id_type=MESH,
        )

    def relay(side, i, ds, dc, h):
        s2, b = at(ds, dc)
        return pltpu.make_async_remote_copy(
            src_ref=kv.at[h, b, :, token_rows(rows, s2), :],
            dst_ref=kv.at[h, b, :, token_rows(halo_base(side), s2), :],
            send_sem=relay_send.at[side, h, i],
            recv_sem=halo_sem.at[side, h, s2, b],
            device_id={"frame": neighbour(side)}, device_id_type=MESH,
        )

    def crosses(side, s2, h, core):
        return (h < full(core)) | (s2 == (S - 1 if side == 0 else 0))

    def send_out(ds, h):
        s2 = lax.rem(s + ds, S)
        return pltpu.make_async_remote_copy(
            src_ref=gb.at[h, token_rows(0, s2), :],
            dst_ref=every.at[rank(h, s, c)],
            send_sem=out_send.at[h, ds - 1],
            recv_sem=out_sem.at[rank(h, s, c)],
            device_id={"seq": s2}, device_id_type=MESH,
        )

    def send_core(h, s2, dc, src):
        return pltpu.make_async_remote_copy(
            src_ref=src,
            dst_ref=every.at[rank(h, s2, c)],
            send_sem=core_send.at[h, s2, dc - 1],
            recv_sem=out_sem.at[rank(h, s2, c)],
            device_id={"cfg": lax.rem(c + dc, C)}, device_id_type=MESH,
        )

    def send_local(h, s2, dc):
        c2 = lax.rem(c + dc, C)
        return pltpu.make_async_remote_copy(
            src_ref=x_ref.at[rank(h, s2, c2)],
            dst_ref=lb.at[h - low, s2, c],
            send_sem=l_send.at[h - low, s2, dc],
            recv_sem=l_sem.at[h - low, s2, c],
            device_id={"cfg": c2}, device_id_type=MESH,
        )

    def own_local(h, s2):
        return pltpu.make_async_copy(
            x_ref.at[rank(h, s2, c)], lb.at[h - low, s2, c], l_sem.at[h - low, s2, c]
        )

    def recv(ref, sem):
        pltpu.make_async_remote_copy(
            src_ref=ref, dst_ref=ref, send_sem=sem, recv_sem=sem,
            device_id={"seq": s}, device_id_type=MESH,
        ).wait_recv()

    sides = ((0, up_ok), (1, down_ok))

    def each_partner(h, act):
        for i, (ds, dc) in enumerate(partners):
            @pl.when(h < shared(lax.rem(c + dc, C)))
            def _():
                act(i, ds, dc, h)

    def each_halo(h, act):
        for side, ok in sides:
            for dc in range(C):
                c2 = lax.rem(c + dc, C)

                @pl.when(ok & (h < shared(c2)) & crosses(side, s, h, c2))
                def _():
                    act(send_halo(side, dc, h))

    def each_relay(i, ds, dc, h, act):
        s2, b = at(ds, dc)
        for side, ok in sides:
            @pl.when(ok & crosses(side, s2, h, c))
            def _():
                act(relay(side, i, ds, dc, h))

    def each_local(act):
        @pl.loop(low, heads)
        def _(h):
            for s2 in range(S):
                for dc in range(1, C):
                    @pl.when(h >= shared(lax.rem(c + dc, C)))
                    def _():
                        act(send_local(h, s2, dc))

    @pl.loop(0, near)
    def _(h):
        each_partner(h, lambda *k: send_kv(*k).start())
        each_halo(h, lambda copy: copy.start())

        @pl.when(h < shared(c))
        def _():
            own_kv(h).start()

    each_local(lambda copy: copy.start())

    @pl.loop(shared(c), heads)
    def _(h):
        for s2 in range(S):
            own_local(h, s2).start()

    @pl.loop(0, near)
    def _(h):
        each_partner(h, lambda *k: send_q(*k).start())

        @pl.when(h < shared(c))
        def _():
            own_q(h).start()

    for edge, base in ((f == 0, 0), (f == F - 1, 2 * rows)):
        @pl.when(edge)
        def _():
            @pl.loop(0, near)
            def _(h):
                kv[h, :, :, pl.ds(base, rows), :] = jnp.zeros((C, 2, rows, HD), kv.dtype)

    many = [jnp.int32(0)] * (W_MAX + 1)
    for head in range(heads * groups):
        for level in range(W_MAX + 1):
            many[level] = many[level] + jnp.where(win_ref[head] >= level, 1, 0)
    place = [many[level + 1] if level < W_MAX else jnp.int32(0) for level in range(W_MAX + 1)]
    for head in range(heads * groups):
        mine = place[0]
        for level in range(1, W_MAX + 1):
            mine = jnp.where(win_ref[head] == level, place[level], mine)
        rank_ref[head] = mine
        for level in range(W_MAX + 1):
            place[level] = place[level] + jnp.where(win_ref[head] == level, 1, 0)

    now = jnp.full((1, HD), time_ref[0], jnp.int32).astype(jnp.float32)
    strength = 1.0 + 4.0 * now / 999.0
    factor = LOG2E / math.sqrt(HD)

    def attend(query, keys, values, bias):
        scores = lax.dot_general(
            query, keys, (((1,), (1,)), ((), ())), preferred_element_type=jnp.float32
        )
        if bias is not None:
            scores = scores + bias
        top = jnp.max(scores, axis=1, keepdims=True)
        expd = jnp.exp2((scores - top) * factor)
        total = jnp.sum(expd, axis=1, keepdims=True)
        part = jnp.dot(expd.astype(jnp.bfloat16), values, preferred_element_type=jnp.float32)
        return (part / total).astype(jnp.bfloat16).astype(jnp.float32)

    def guide(cond, uncond):
        return (uncond + strength * (cond - uncond)).astype(jnp.bfloat16)

    @pl.loop(shared(c), heads)
    def _(h):
        for s2 in range(S):
            own_local(h, s2).wait()
            for dc in range(1, C):
                b = lax.rem(c + dc, C)
                recv(lb.at[h - low, s2, b], l_sem.at[h - low, s2, b])
            cond, uncond = [
                attend(lb[h - low, s2, b, 0], lb[h - low, s2, b, 1], lb[h - low, s2, b, 2], None)
                for b in range(C)
            ]
            every[rank(h, s2, c)] = guide(cond, uncond)
            for dc in range(1, C):
                send_core(h, s2, dc, every.at[rank(h, s2, c)]).start()

    @pl.loop(0, shared(c))
    def _(h):
        for i, ds, dc in others:
            s2, b = at(ds, dc)
            recv(kv.at[h, b, :, token_rows(rows, s2), :], kv_sem.at[h, s2, b])
            each_relay(i, ds, dc, h, lambda copy: copy.start())

    def hand_on(h):
        for ds in range(1, S):
            s2 = lax.rem(s + ds, S)
            ref = every.at[rank(h, s2, c)]
            recv(ref, out_sem.at[rank(h, s2, c)])
            for dc in range(1, C):
                send_core(h, s2, dc, ref).start()

    for lo, hi, reach in ((0, full(c), W_MAX), (full(c), shared(c), 1)):
        @pl.loop(lo, hi)
        def _(h):
            own_kv(h).wait()
            own_q(h).wait()
            for ds, dc in partners:
                s2, b = at(ds, dc)
                if not ds:
                    recv(kv.at[h, b, :, token_rows(rows, s2), :], kv_sem.at[h, s2, b])
                recv(qb.at[h, b, token_rows(0, s2), :], q_sem.at[h, s2, b])
            for side, ok in ((0, down_ok), (1, up_ok)):
                for ds in range(S):
                    s2 = lax.rem(s + ds, S)

                    @pl.when(ok & crosses(side, s2, h, c))
                    def _():
                        for b in range(C):
                            recv(
                                kv.at[h, b, :, token_rows(halo_base(side), s2), :],
                                halo_sem.at[side, h, s2, b],
                            )
            me = rank(h, s, c)
            window = jnp.int32(0)
            for level in range(1, W_MAX + 1):
                window = window + jnp.where(me < many[level], 1, 0)
            for number in range(frames_here):
                here = f * frames_here + number
                own_shot = seg_ref[here]
                pieces = []
                for offset in range(-reach, reach + 1):
                    there = here + offset
                    shot = seg_ref[jnp.clip(there, 0, frames - 1)]
                    allowed = (
                        (there >= 0) & (there < frames)
                        & (shot == own_shot) & (abs(offset) <= window)
                    )
                    pieces.append(
                        jnp.full((1, per_frame), jnp.where(allowed, 0.0, NEG), jnp.float32)
                    )
                bias = jnp.concatenate(pieces, axis=1)
                keys = pl.ds((frames_here + number - reach) * per_frame, len(pieces) * per_frame)
                mine = pl.ds(number * per_frame, per_frame)
                cond, uncond = [
                    attend(qb[h, b, mine, :], kv[h, b, 0, keys, :], kv[h, b, 1, keys, :], bias)
                    for b in range(C)
                ]
                gb[h, mine, :] = guide(cond, uncond)
            for ds in range(1, S):
                send_out(ds, h).start()
            for dc in range(1, C):
                send_core(h, s, dc, gb.at[h, token_rows(0, s), :]).start()
            every[me] = gb[h, token_rows(0, s), :]

            @pl.when(h > 0)
            def _():
                hand_on(h - 1)

    hand_on(shared(c) - 1)

    @pl.loop(0, near)
    def _(h):
        each_partner(h, lambda *k: send_kv(*k).wait_send())
        each_partner(h, lambda *k: send_q(*k).wait_send())
        each_halo(h, lambda copy: copy.wait_send())

    @pl.loop(0, shared(c))
    def _(h):
        for i, ds, dc in others:
            each_relay(i, ds, dc, h, lambda copy: copy.wait_send())

    each_local(lambda copy: copy.wait_send())

    @pl.loop(0, heads)
    def _(h):
        for s2 in range(S):
            for dc in range(1, C):
                r = rank(h, s2, lax.rem(c + dc, C))
                recv(every.at[r], out_sem.at[r])

    half = heads
    for s2 in range(S):
        for i in range(half):
            head = s2 * (C * half) + c * half + i
            out_ref[i, :, s2 * HD : (s2 + 1) * HD] = every[rank_ref[head]]

    @pl.loop(0, shared(c))
    def _(h):
        for ds in range(1, S):
            send_out(ds, h).wait_send()

    @pl.loop(0, heads)
    def _(h):
        for s2 in range(S):
            for dc in range(1, C):
                send_core(h, s2, dc, every.at[rank(h, s2, c)]).wait_send()


def plan_kernel(heads_all, levels, room, win_ref, plan_ref, fits_ref):
    many = [jnp.int32(0)] * (levels + 2)
    for head in range(heads_all):
        for level in range(1, levels + 1):
            many[level] = many[level] + (win_ref[head] >= level).astype(jnp.int32)
    fits = jnp.int32(1)
    for level in range(1, levels + 1):
        plan_ref[2 * heads_all + level - 1] = many[level]
        fits = fits * (many[level] <= room[level - 1]).astype(jnp.int32)
    fits_ref[0] = fits
    place = [many[level + 1] for level in range(levels + 1)]
    for head in range(heads_all):
        slot = place[0]
        for level in range(1, levels + 1):
            slot = jnp.where(win_ref[head] == level, place[level], slot)
        for level in range(levels + 1):
            place[level] = place[level] + (win_ref[head] == level).astype(jnp.int32)
        plan_ref[slot] = head
        plan_ref[heads_all + head] = slot


def fast_kernel(
    dims, x_ref, plan_ref, time_ref, seg_ref, out_ref,
    xq, xk, xv, qs, kw, qv, qr, tb, tr, ts, tsr, oh, ohr, hs, hr, ov, ovr, vs, ws, wr, gs, gr, every,
    la, lr,
    load_sem, q_send, q_recv, f_send, f_recv, t_send, t_recv, k_send, k_recv, s_send, s_recv,
    c_send, c_recv, w_send, w_recv, g_send, g_recv, h_send, h_recv, e_send, e_recv,
    l_send, l_recv,
):
    F, heads_all, W, M, tl = dims
    N = M - W
    L = heads_all - M
    s = lax.axis_index("seq")
    c = lax.axis_index("cfg")
    f = lax.axis_index("frame")
    frames = 2 * F
    dz = 1 - 2 * s
    up_ok, down_ok = f < F - 1, f > 0
    fwd, back = f + dz, f - dz
    fwd_ok = (fwd >= 0) & (fwd < F)
    back_ok = (back >= 0) & (back < F)
    lanes = [slice(128 * j, 128 * (j + 1)) for j in range(tl // 128)]
    k = len(lanes)

    barrier = pltpu.get_barrier_semaphore()
    for axis, other in (("seq", 1 - s), ("cfg", 1 - c)):
        pl.semaphore_signal(barrier, inc=1, device_id={axis: other}, device_id_type=MESH)
    for ok, step in ((up_ok, 1), (down_ok, -1)):
        @pl.when(ok)
        def _():
            pl.semaphore_signal(
                barrier, inc=1, device_id={"frame": f + step}, device_id_type=MESH
            )

    own = (xq, xk, xv)
    for part, ref in enumerate(own):
        @pl.loop(0, heads_all)
        def _(h):
            pltpu.make_async_copy(
                x_ref.at[part, :, pl.ds(pl.multiple_of(h * HD, HD), HD)], ref.at[h],
                load_sem.at[part],
            ).start()

    def loaded(part):
        pltpu.make_async_copy(own[part], own[part], load_sem.at[part]).wait()

    def remote(src, dst, send, arrive, where):
        return pltpu.make_async_remote_copy(
            src_ref=src, dst_ref=dst, send_sem=send, recv_sem=arrive,
            device_id=where, device_id_type=MESH,
        )

    across = {"seq": 1 - s}
    beside = {"cfg": 1 - c}

    def send_q(i):
        return remote(qs.at[i], qv.at[i], q_send.at[i], q_recv.at[i], across)

    def send_fwd(n):
        return remote(qv.at[W + n], qr.at[n], f_send.at[n], f_recv.at[n], {"frame": fwd})

    def send_third(n):
        return (
            remote(tb.at[n], tr.at[n], t_send.at[0, n], t_recv.at[0, n], {"frame": back}),
            remote(ts.at[n], tsr.at[n], t_send.at[1, n], t_recv.at[1, n], {"frame": back}),
        )

    def send_kv(side, i):
        start = 0 if side == 0 else 2 * tl
        return remote(
            kw.at[i, :, pl.ds(tl, tl), :], kw.at[i, :, pl.ds(start, tl), :],
            k_send.at[side, i], k_recv.at[side, i], {"frame": f + 1 if side == 0 else f - 1},
        )

    def send_stats(i):
        return remote(hs.at[i], hr.at[i], s_send.at[i], s_recv.at[i], across)

    def send_near_stats():
        part = pl.ds(W, N)
        return remote(hs.at[part], hr.at[part], s_send.at[W], s_recv.at[W], across)

    def send_part(i):
        return remote(ov.at[i], ovr.at[i], c_send.at[i], c_recv.at[i], beside)

    def send_weight(i):
        return remote(ws.at[i], wr.at[i], w_send.at[i], w_recv.at[i], across)

    def send_guided(i):
        return remote(gs.at[i], gr.at[i], g_send.at[i], g_recv.at[i], across)

    def send_home(i):
        return remote(oh.at[i], ohr.at[i], h_send.at[i], h_recv.at[i], beside)

    def send_final(i):
        return remote(every.at[i], every.at[i], e_send.at[i], e_recv.at[i], beside)

    def send_local(n):
        return remote(la.at[n], lr.at[n], l_send.at[n], l_recv.at[n], beside)

    def mine(i):
        return lax.rem(i, 2) == c

    factor = LOG2E / math.sqrt(HD)
    rows_id = lax.broadcasted_iota(jnp.int32, (128, 128), 0)
    lanes_id = lax.broadcasted_iota(jnp.int32, (128, 128), 1)
    eye = rows_id == lanes_id
    now = jnp.full((1, HD), time_ref[0], jnp.int32).astype(jnp.float32)
    strength = 1.0 + 4.0 * now / 999.0
    coef = jnp.where(c == 0, strength, 1.0 - strength)

    def to_row(column):
        return [
            jnp.sum(jnp.where(eye, column[part], 0.0), axis=0, keepdims=True) for part in lanes
        ]

    def to_column(row):
        return jnp.concatenate(
            [
                jnp.sum(jnp.where(eye, row[j : j + 1], 0.0), axis=1, keepdims=True)
                for j in range(k)
            ],
            axis=0,
        )

    def attend(query, keys, values, bias=None):
        scores = lax.dot_general(
            query, keys, (((1,), (1,)), ((), ())), preferred_element_type=jnp.float32
        )
        if bias is not None:
            scores = scores + bias
        top = jnp.max(scores, axis=1, keepdims=True)
        expd = jnp.exp2((scores - top) * factor)
        total = jnp.sum(expd, axis=1, keepdims=True)
        part = jnp.dot(expd.astype(jnp.bfloat16), values, preferred_element_type=jnp.float32)
        return part / total, top, total

    def keep_stats(ref, i, top, total):
        for j, row in enumerate(to_row(top) + to_row(total)):
            ref[i, j : j + 1, :] = row

    me = 2 * f + s
    visitor = 2 * f + 1 - s
    beyond = me + 2 * dz

    def shot(frame):
        return seg_ref[jnp.clip(frame, 0, frames - 1)]

    same_visit = shot(me) == shot(visitor)
    same_beyond = fwd_ok & (shot(visitor) == shot(beyond))
    same_low = down_ok & (shot(me) == shot(me - 2))
    same_high = up_ok & (shot(me) == shot(me + 2))

    def reach(level, i):
        return i < plan_ref[2 * heads_all + level - 1]

    def piece(allowed):
        return jnp.full((1, tl), jnp.where(allowed, 0.0, NEG), jnp.float32)

    loaded(0)

    @pl.loop(0, M)
    def _(i):
        qs[i] = xq[plan_ref[i]]

    pl.semaphore_wait(
        barrier, 2 + jnp.where(up_ok, 1, 0) + jnp.where(down_ok, 1, 0)
    )

    @pl.loop(W, M)
    def _(i):
        send_q(i).start()

    loaded(1)
    loaded(2)

    @pl.loop(0, W)
    def _(i):
        for part in range(2):
            kw[i, part, pl.ds(tl, tl), :] = own[1 + part][plan_ref[i]]

    first_kv = [jnp.where(s == side, DZ_EARLY, BACK_EARLY) for side in range(2)]

    def spread_kv(early):
        for side, ok in ((0, up_ok), (1, down_ok)):
            @pl.when(ok)
            def _():
                @pl.loop(0 if early else first_kv[side], first_kv[side] if early else W)
                def _(i):
                    send_kv(side, i).start()

    spread_kv(True)

    for ok, start in ((down_ok, 0), (up_ok, 2 * tl)):
        @pl.when(jnp.logical_not(ok))
        def _():
            @pl.loop(0, W)
            def _(i):
                kw[i, :, pl.ds(start, tl), :] = jnp.zeros((2, tl, HD), kw.dtype)

    @pl.when(jnp.logical_not(fwd_ok))
    def _():
        @pl.loop(0, N)
        def _(n):
            tr[n] = jnp.zeros((tl, HD), tr.dtype)
            tsr[n] = jnp.zeros((2 * k, 128), tsr.dtype)

    @pl.loop(W, M)
    def _(i):
        here = plan_ref[i]
        out, top, total = attend(qs[i], xk[here], xv[here])
        oh[i] = out
        keep_stats(hs, i, top, total)

    send_near_stats().start()

    @pl.loop(0, W)
    def _(i):
        send_q(i).start()

    LAG = 2

    @pl.loop(0, max(N + LAG, L))
    def _(n):
        @pl.when(n < N)
        def _():
            i = W + n
            send_q(i).wait_recv()

            @pl.when(fwd_ok)
            def _():
                send_fwd(n).start()

            here = plan_ref[i]
            out, top, total = attend(qv[i], xk[here], xv[here])
            ov[i] = out
            keep_stats(vs, i, top, total)

        @pl.when((n >= LAG) & (n < N + LAG) & back_ok)
        def _():
            m = n - LAG
            send_fwd(m).wait_recv()
            here = plan_ref[W + m]
            out, top, total = attend(qr[m], xk[here], xv[here])
            tb[m] = out.astype(jnp.bfloat16)
            keep_stats(ts, m, top, total)
            for copy in send_third(m):
                copy.start()

        @pl.when(n < L)
        def _():
            here = plan_ref[M + n]
            out, _, _ = attend(xq[here], xk[here], xv[here])
            la[n] = out.astype(jnp.bfloat16)
            send_local(n).start()

    spread_kv(False)

    def weigh(i, home, parts):
        tops = [
            ref[at, 0:k, :] + jnp.full((1, 128), jnp.where(ok, 0.0, NEG), jnp.float32)
            for ref, at, ok in parts
        ]
        tops.append(home[i, 0:k, :])
        high = functools.reduce(jnp.maximum, tops)
        sums = [ref[at, k : 2 * k, :] for ref, at, _ in parts] + [home[i, k : 2 * k, :]]
        mass = [jnp.exp2((top - high) * factor) * total for top, total in zip(tops, sums)]
        whole = sum(mass)
        shares = [part / whole for part in mass]
        ws[i] = shares[-1]
        send_weight(i).start()
        return [to_column(share) * coef for share in shares[:-1]]

    def hand_over(i):
        @pl.when(jnp.logical_not(mine(i)))
        def _():
            send_part(i).start()

    def join(i):
        @pl.when(mine(i))
        def _():
            send_part(i).wait_recv()
            gs[i] = (ov[i] + ovr[i]).astype(jnp.bfloat16)
            send_guided(i).start()

    def weigh_home(i):
        send_weight(i).wait_recv()
        oh[i] = oh[i] * (to_column(wr[i]) * coef)

        @pl.when(jnp.logical_not(mine(i)))
        def _():
            send_home(i).start()

    def finish(i):
        @pl.when(mine(i))
        def _():
            send_home(i).wait_recv()
            send_guided(i).wait_recv()
            every[i] = (gr[i].astype(jnp.float32) + oh[i] + ohr[i]).astype(jnp.bfloat16)
            send_final(i).start()

    send_near_stats().wait_recv()

    @pl.loop(0, N)
    def _(n):
        i = W + n

        @pl.when(fwd_ok)
        def _():
            for copy in send_third(n):
                copy.wait_recv()

        near = reach(1, i)
        first, second = weigh(
            i, hr, [(vs, i, near & same_visit), (tsr, n, near & same_beyond)]
        )
        ov[i] = first * ov[i] + second * tr[n].astype(jnp.float32)
        hand_over(i)

    @pl.loop(0, L)
    def _(n):
        send_local(n).wait_recv()
        here, there = la[n].astype(jnp.float32), lr[n].astype(jnp.float32)
        cond = jnp.where(c == 0, here, there)
        uncond = jnp.where(c == 0, there, here)
        every[M + n] = (uncond + strength * (cond - uncond)).astype(jnp.bfloat16)

    first_keys = pl.multiple_of(tl * (1 - s), tl)
    per = -(-N // W)

    @pl.loop(0, W + DONE_LAG)
    def _(j):
        @pl.when(j < W)
        def _():
            send_q(j).wait_recv()

            @pl.when(down_ok)
            def _():
                send_kv(0, j).wait_recv()

            @pl.when(up_ok)
            def _():
                send_kv(1, j).wait_recv()

            wide = reach(2, j)
            near = reach(1, j)
            bias = jnp.concatenate(
                [piece(wide & same_low), piece(True), piece(wide & same_high)], axis=1
            )
            out, top, total = attend(qs[j], kw[j, 0], kw[j, 1], bias)
            oh[j] = out
            keep_stats(hs, j, top, total)
            send_stats(j).start()
            one = near & same_visit
            two = near & same_beyond
            bias = jnp.concatenate(
                [
                    piece(jnp.where(s == 0, one, two)),
                    piece(jnp.where(s == 0, two, one)),
                ],
                axis=1,
            )
            keys = pl.ds(first_keys, 2 * tl)
            out, top, total = attend(qv[j], kw[j, 0, keys, :], kw[j, 1, keys, :], bias)
            ov[j] = out
            keep_stats(vs, j, top, total)

        @pl.when((j >= HOST_LAG) & (j < W + HOST_LAG))
        def _():
            m = j - HOST_LAG
            send_stats(m).wait_recv()
            (share,) = weigh(m, hr, [(vs, m, reach(1, m) & (same_visit | same_beyond))])
            ov[m] = share * ov[m]
            hand_over(m)

        for part in range(per):
            n = per * j + part

            @pl.when(n < N)
            def _():
                join(W + n)

            late = per * (j - NEAR_HOME_LAG) + part

            @pl.when((late >= 0) & (late < N))
            def _():
                weigh_home(W + late)

        @pl.when((j >= JOIN_LAG) & (j < W + JOIN_LAG))
        def _():
            join(j - JOIN_LAG)

        @pl.when((j >= HOME_LAG) & (j < W + HOME_LAG))
        def _():
            weigh_home(j - HOME_LAG)

        for part in range(per):
            late = per * (j - NEAR_DONE_LAG) + part

            @pl.when((late >= 0) & (late < N))
            def _():
                finish(W + late)

        @pl.when(j >= DONE_LAG)
        def _():
            finish(j - DONE_LAG)

    @pl.loop(0, M)
    def _(i):
        @pl.when(jnp.logical_not(mine(i)))
        def _():
            send_final(i).wait_recv()

    half = heads_all // 4
    for s2 in range(2):
        for i in range(half):
            head = s2 * (2 * half) + c * half + i
            out_ref[i, :, s2 * HD : (s2 + 1) * HD] = every[plan_ref[heads_all + head]]

    @pl.loop(0, M)
    def _(i):
        send_q(i).wait_send()
        send_weight(i).wait_send()

        @pl.when(mine(i))
        def _():
            send_guided(i).wait_send()
            send_final(i).wait_send()

        @pl.when(jnp.logical_not(mine(i)))
        def _():
            send_part(i).wait_send()
            send_home(i).wait_send()

    @pl.loop(0, N)
    def _(n):
        @pl.when(fwd_ok)
        def _():
            send_fwd(n).wait_send()

        @pl.when(back_ok)
        def _():
            for copy in send_third(n):
                copy.wait_send()

    send_near_stats().wait_send()

    @pl.loop(0, W)
    def _(i):
        send_stats(i).wait_send()
        for side, ok in ((0, up_ok), (1, down_ok)):
            @pl.when(ok)
            def _():
                send_kv(side, i).wait_send()

    @pl.loop(0, L)
    def _(n):
        send_local(n).wait_send()


def fast_call(F, heads_all, W, M, tl, number):
    N, L, k = M - W, heads_all - M, tl // 128
    dma = pltpu.SemaphoreType.DMA

    def block(count, dtype=jnp.bfloat16):
        return pltpu.VMEM((count, tl, HD), dtype)

    def small(count, rows):
        return pltpu.VMEM((count, rows, 128), jnp.float32)

    f32 = jnp.float32
    return pl.pallas_call(
        functools.partial(fast_kernel, (F, heads_all, W, M, tl)),
        out_shape=jax.ShapeDtypeStruct((heads_all // 4, tl, 2 * HD), jnp.bfloat16),
        in_specs=[pl.BlockSpec(memory_space=pl.ANY)]
        + [pl.BlockSpec(memory_space=pltpu.SMEM)] * 3,
        out_specs=pl.BlockSpec(memory_space=pltpu.VMEM),
        scratch_shapes=[
            block(heads_all), block(heads_all), block(heads_all),
            block(M), pltpu.VMEM((W, 2, 3 * tl, HD), jnp.bfloat16), block(M),
            block(N), block(N), block(N), small(N, 2 * k), small(N, 2 * k),
            block(M, f32), block(M, f32), small(M, 2 * k), small(M, 2 * k),
            block(M, f32), block(M, f32), small(M, 2 * k), small(M, k), small(M, k),
            block(M), block(M), block(heads_all), block(L), block(L),
            dma((3,)), dma((M,)), dma((M,)), dma((N,)), dma((N,)), dma((2, N)), dma((2, N)),
            dma((2, W)), dma((2, W)), dma((W + 1,)), dma((W + 1,)),
            dma((M,)), dma((M,)), dma((M,)), dma((M,)), dma((M,)), dma((M,)),
            dma((M,)), dma((M,)), dma((M,)), dma((M,)), dma((L,)), dma((L,)),
        ],
        compiler_params=pltpu.CompilerParams(
            collective_id=number, has_side_effects=True, vmem_limit_bytes=56 * 2**20
        ),
        name=f"visiting_attention_{number}",
    )


def body(qkv, timestep, windows, segments):
    S, C, F = (lax.axis_size(axis) for axis in ("seq", "cfg", "frame"))
    x = jnp.transpose(qkv[0], (1, 0, 2))
    tl = x.shape[1]
    heads = x.shape[2] // HD // (S * C)
    frames_here = segments.shape[0] // F
    assert frames_here == W_MAX and heads * S * C * HD == x.shape[2]
    rows = S * tl
    groups = S * C
    n = groups - 1
    dma = pltpu.SemaphoreType.DMA
    heads_all = heads * groups

    def general(x, timestep, windows, segments):
        ordered, _ = pl.pallas_call(
            functools.partial(gather_kernel, heads_all, W_MAX, (heads_all,) * W_MAX),
            out_shape=(
                jax.ShapeDtypeStruct((heads_all, 3, tl, HD), x.dtype),
                jax.ShapeDtypeStruct((1,), jnp.int32),
            ),
            in_specs=[pl.BlockSpec(memory_space=pl.ANY), pl.BlockSpec(memory_space=pltpu.SMEM)],
            out_specs=(
                pl.BlockSpec(memory_space=pltpu.VMEM),
                pl.BlockSpec(memory_space=pltpu.SMEM),
            ),
            scratch_shapes=[dma],
            name="order_heads",
            compiler_params=pltpu.CompilerParams(vmem_limit_bytes=56 * 2**20),
        )(x, windows)
        kept, near = 1, heads
        return pl.pallas_call(
            functools.partial(kernel, (S, C, F, heads, tl, frames_here, heads, heads, 0)),
            out_shape=jax.ShapeDtypeStruct((heads, tl, S * HD), jnp.bfloat16),
            in_specs=[pl.BlockSpec(memory_space=pl.ANY)]
            + [pl.BlockSpec(memory_space=pltpu.SMEM)] * 3,
            out_specs=pl.BlockSpec(memory_space=pltpu.VMEM),
            scratch_shapes=[
                pltpu.VMEM((near, C, 2, 3 * rows, HD), jnp.bfloat16),
                pltpu.VMEM((near, C, rows, HD), jnp.bfloat16),
                pltpu.VMEM((near, rows, HD), jnp.bfloat16),
                pltpu.VMEM((kept, S, C, 3, tl, HD), jnp.bfloat16),
                pltpu.VMEM((heads_all, tl, HD), jnp.bfloat16),
                pltpu.SMEM((heads_all,), jnp.int32),
                dma((near, S, C)),
                dma((near, S, C)),
                dma((2, near, S, C)),
                dma((heads_all,)),
                dma((2, near, n)),
                dma((2, near, C)),
                dma((2, near, n)),
                dma((near, max(S - 1, 1))),
                dma((heads, S, C - 1)),
                dma((kept, S, C)),
                dma((kept, S, C)),
            ],
            compiler_params=pltpu.CompilerParams(
                collective_id=0, has_side_effects=True, vmem_limit_bytes=40 * 2**20
            ),
            name="guided_attention_0",
        )(ordered, timestep, windows, segments)

    if S == C == frames_here == 2 and tl % 128 == 0 and heads_all >= 8:
        wide, near = heads_all // 3, 2 * heads_all // 3
        plan, fits = pl.pallas_call(
            functools.partial(plan_kernel, heads_all, W_MAX, (near, wide)),
            out_shape=(
                jax.ShapeDtypeStruct((2 * heads_all + W_MAX,), jnp.int32),
                jax.ShapeDtypeStruct((1,), jnp.int32),
            ),
            in_specs=[pl.BlockSpec(memory_space=pltpu.SMEM)],
            out_specs=(pl.BlockSpec(memory_space=pltpu.SMEM),) * 2,
            name="plan_heads",
        )(windows)

        def fast(x, plan, timestep, windows, segments):
            return fast_call(F, heads_all, wide, near, tl, 1)(x, plan, timestep, segments)

        def slow(x, plan, timestep, windows, segments):
            return general(x, timestep, windows, segments)

        out = lax.cond(fits[0] > 0, fast, slow, x, plan, timestep, windows, segments)
    else:
        out = general(x, timestep, windows, segments)
    return jnp.transpose(out, (1, 0, 2))


def solution(mesh):
    return jax.shard_map(
        body,
        mesh=mesh,
        in_specs=(P("cfg", ("groups", "frame", "seq"), None, None), P("groups"), P(), P("groups")),
        out_specs=P(("groups", "frame", "seq"), "cfg", None),
        check_vma=False,
    )
```

```python
import functools
import math

import jax
import jax.numpy as jnp
from jax import lax
from jax.experimental import pallas as pl
from jax.experimental.pallas import tpu as pltpu
from jax.sharding import PartitionSpec as P

HD = 128
W_MAX = 2
NEG = -1e30
LOG2E = 1.4426950408889634
MESH = pl.DeviceIdType.MESH
DZ_EARLY, BACK_EARLY = 2, 3
HOST_LAG, JOIN_LAG, HOME_LAG, DONE_LAG = 2, 3, 5, 6
NEAR_HOME_LAG, NEAR_DONE_LAG = 2, 3


def gather_kernel(heads_all, levels, room, x_ref, win_ref, out_ref, fits_ref, sem):
    def copy(head, slot):
        return pltpu.make_async_copy(
            x_ref.at[:, :, pl.ds(pl.multiple_of(head * HD, HD), HD)], out_ref.at[slot], sem
        )

    def place(level):
        def step(head, slot):
            hit = win_ref[head] == level

            @pl.when(hit)
            def _():
                copy(head, slot).start()

            return slot + hit.astype(jnp.int32)

        return step

    slot = jnp.int32(0)
    fits = jnp.int32(1)
    for level in range(levels, -1, -1):
        slot = lax.fori_loop(0, heads_all, place(level), slot)
        if level:
            fits = fits * (slot <= room[level - 1]).astype(jnp.int32)
    fits_ref[0] = fits
    pltpu.make_async_copy(out_ref, out_ref, sem).wait()


def kernel(
    dims, x_ref, time_ref, win_ref, seg_ref, out_ref,
    kv, qb, gb, lb, every, rank_ref,
    kv_sem, q_sem, halo_sem, out_sem, a2a_send, own_send, relay_send, out_send, core_send,
    l_sem, l_send,
):
    S, C, F, heads, tl, frames_here, wide, near, short = dims
    groups = S * C
    rows = S * tl
    per_frame = rows // frames_here
    frames = F * frames_here
    s = lax.axis_index("seq")
    c = lax.axis_index("cfg")
    f = lax.axis_index("frame")
    partners = [(ds, dc) for ds in range(S) for dc in range(C) if ds or dc]
    others = [(i, ds, dc) for i, (ds, dc) in enumerate(partners) if ds]
    up_ok = f < F - 1
    down_ok = f > 0

    def at(ds, dc):
        return lax.rem(s + ds, S), lax.rem(c + dc, C)

    def rank(h, s2, c2):
        return h * groups + c2 * S + s2

    def token_rows(base, piece):
        return pl.ds(pl.multiple_of(base + piece * tl, tl), tl)

    def full(core):
        return wide - jnp.where(core > 0, short, 0)

    def shared(core):
        return near - jnp.where(core > 0, short, 0)

    low = near - short

    barrier = pltpu.get_barrier_semaphore()
    for ds, dc in partners:
        s2, c2 = at(ds, dc)
        pl.semaphore_signal(
            barrier, inc=1, device_id={"seq": s2, "cfg": c2}, device_id_type=MESH
        )
    for step in (-1, 1):
        @pl.when((f + step >= 0) & (f + step < F))
        def _():
            for dc in range(C):
                pl.semaphore_signal(
                    barrier, inc=1,
                    device_id={"frame": f + step, "cfg": lax.rem(c + dc, C)},
                    device_id_type=MESH,
                )
    beside = jnp.where(f > 0, C, 0) + jnp.where(f < F - 1, C, 0)
    pl.semaphore_wait(barrier, len(partners) + beside)

    def send_kv(i, ds, dc, h):
        s2, c2 = at(ds, dc)
        return pltpu.make_async_remote_copy(
            src_ref=x_ref.at[rank(h, s2, c2), pl.ds(1, 2)],
            dst_ref=kv.at[h, c, :, token_rows(rows, s), :],
            send_sem=a2a_send.at[0, h, i],
            recv_sem=kv_sem.at[h, s, c],
            device_id={"seq": s2, "cfg": c2}, device_id_type=MESH,
        )

    def send_q(i, ds, dc, h):
        s2, c2 = at(ds, dc)
        return pltpu.make_async_remote_copy(
            src_ref=x_ref.at[rank(h, s2, c2), 0],
            dst_ref=qb.at[h, c, token_rows(0, s), :],
            send_sem=a2a_send.at[1, h, i],
            recv_sem=q_sem.at[h, s, c],
            device_id={"seq": s2, "cfg": c2}, device_id_type=MESH,
        )

    def own_kv(h):
        return pltpu.make_async_copy(
            x_ref.at[rank(h, s, c), pl.ds(1, 2)],
            kv.at[h, c, :, token_rows(rows, s), :],
            kv_sem.at[h, s, c],
        )

    def own_q(h):
        return pltpu.make_async_copy(
            x_ref.at[rank(h, s, c), 0], qb.at[h, c, token_rows(0, s), :], q_sem.at[h, s, c]
        )

    def halo_base(side):
        return 0 if side == 0 else 2 * rows

    def neighbour(side):
        return f + (1 if side == 0 else -1)

    def send_halo(side, dc, h):
        c2 = lax.rem(c + dc, C)
        return pltpu.make_async_remote_copy(
            src_ref=x_ref.at[rank(h, s, c2), pl.ds(1, 2)],
            dst_ref=kv.at[h, c, :, token_rows(halo_base(side), s), :],
            send_sem=own_send.at[side, h, dc],
            recv_sem=halo_sem.at[side, h, s, c],
            device_id={"frame": neighbour(side), "cfg": c2}, device_id_type=MESH,
        )

    def relay(side, i, ds, dc, h):
        s2, b = at(ds, dc)
        return pltpu.make_async_remote_copy(
            src_ref=kv.at[h, b, :, token_rows(rows, s2), :],
            dst_ref=kv.at[h, b, :, token_rows(halo_base(side), s2), :],
            send_sem=relay_send.at[side, h, i],
            recv_sem=halo_sem.at[side, h, s2, b],
            device_id={"frame": neighbour(side)}, device_id_type=MESH,
        )

    def crosses(side, s2, h, core):
        return (h < full(core)) | (s2 == (S - 1 if side == 0 else 0))

    def send_out(ds, h):
        s2 = lax.rem(s + ds, S)
        return pltpu.make_async_remote_copy(
            src_ref=gb.at[h, token_rows(0, s2), :],
            dst_ref=every.at[rank(h, s, c)],
            send_sem=out_send.at[h, ds - 1],
            recv_sem=out_sem.at[rank(h, s, c)],
            device_id={"seq": s2}, device_id_type=MESH,
        )

    def send_core(h, s2, dc, src):
        return pltpu.make_async_remote_copy(
            src_ref=src,
            dst_ref=every.at[rank(h, s2, c)],
            send_sem=core_send.at[h, s2, dc - 1],
            recv_sem=out_sem.at[rank(h, s2, c)],
            device_id={"cfg": lax.rem(c + dc, C)}, device_id_type=MESH,
        )

    def send_local(h, s2, dc):
        c2 = lax.rem(c + dc, C)
        return pltpu.make_async_remote_copy(
            src_ref=x_ref.at[rank(h, s2, c2)],
            dst_ref=lb.at[h - low, s2, c],
            send_sem=l_send.at[h - low, s2, dc],
            recv_sem=l_sem.at[h - low, s2, c],
            device_id={"cfg": c2}, device_id_type=MESH,
        )

    def own_local(h, s2):
        return pltpu.make_async_copy(
            x_ref.at[rank(h, s2, c)], lb.at[h - low, s2, c], l_sem.at[h - low, s2, c]
        )

    def recv(ref, sem):
        pltpu.make_async_remote_copy(
            src_ref=ref, dst_ref=ref, send_sem=sem, recv_sem=sem,
            device_id={"seq": s}, device_id_type=MESH,
        ).wait_recv()

    sides = ((0, up_ok), (1, down_ok))

    def each_partner(h, act):
        for i, (ds, dc) in enumerate(partners):
            @pl.when(h < shared(lax.rem(c + dc, C)))
            def _():
                act(i, ds, dc, h)

    def each_halo(h, act):
        for side, ok in sides:
            for dc in range(C):
                c2 = lax.rem(c + dc, C)

                @pl.when(ok & (h < shared(c2)) & crosses(side, s, h, c2))
                def _():
                    act(send_halo(side, dc, h))

    def each_relay(i, ds, dc, h, act):
        s2, b = at(ds, dc)
        for side, ok in sides:
            @pl.when(ok & crosses(side, s2, h, c))
            def _():
                act(relay(side, i, ds, dc, h))

    def each_local(act):
        @pl.loop(low, heads)
        def _(h):
            for s2 in range(S):
                for dc in range(1, C):
                    @pl.when(h >= shared(lax.rem(c + dc, C)))
                    def _():
                        act(send_local(h, s2, dc))

    @pl.loop(0, near)
    def _(h):
        each_partner(h, lambda *k: send_kv(*k).start())
        each_halo(h, lambda copy: copy.start())

        @pl.when(h < shared(c))
        def _():
            own_kv(h).start()

    each_local(lambda copy: copy.start())

    @pl.loop(shared(c), heads)
    def _(h):
        for s2 in range(S):
            own_local(h, s2).start()

    @pl.loop(0, near)
    def _(h):
        each_partner(h, lambda *k: send_q(*k).start())

        @pl.when(h < shared(c))
        def _():
            own_q(h).start()

    for edge, base in ((f == 0, 0), (f == F - 1, 2 * rows)):
        @pl.when(edge)
        def _():
            @pl.loop(0, near)
            def _(h):
                kv[h, :, :, pl.ds(base, rows), :] = jnp.zeros((C, 2, rows, HD), kv.dtype)

    many = [jnp.int32(0)] * (W_MAX + 1)
    for head in range(heads * groups):
        for level in range(W_MAX + 1):
            many[level] = many[level] + jnp.where(win_ref[head] >= level, 1, 0)
    place = [many[level + 1] if level < W_MAX else jnp.int32(0) for level in range(W_MAX + 1)]
    for head in range(heads * groups):
        mine = place[0]
        for level in range(1, W_MAX + 1):
            mine = jnp.where(win_ref[head] == level, place[level], mine)
        rank_ref[head] = mine
        for level in range(W_MAX + 1):
            place[level] = place[level] + jnp.where(win_ref[head] == level, 1, 0)

    now = jnp.full((1, HD), time_ref[0], jnp.int32).astype(jnp.float32)
    strength = 1.0 + 4.0 * now / 999.0
    factor = LOG2E / math.sqrt(HD)

    def attend(query, keys, values, bias):
        scores = lax.dot_general(
            query, keys, (((1,), (1,)), ((), ())), preferred_element_type=jnp.float32
        )
        if bias is not None:
            scores = scores + bias
        top = jnp.max(scores, axis=1, keepdims=True)
        expd = jnp.exp2((scores - top) * factor)
        total = jnp.sum(expd, axis=1, keepdims=True)
        part = jnp.dot(expd.astype(jnp.bfloat16), values, preferred_element_type=jnp.float32)
        return (part / total).astype(jnp.bfloat16).astype(jnp.float32)

    def guide(cond, uncond):
        return (uncond + strength * (cond - uncond)).astype(jnp.bfloat16)

    @pl.loop(shared(c), heads)
    def _(h):
        for s2 in range(S):
            own_local(h, s2).wait()
            for dc in range(1, C):
                b = lax.rem(c + dc, C)
                recv(lb.at[h - low, s2, b], l_sem.at[h - low, s2, b])
            cond, uncond = [
                attend(lb[h - low, s2, b, 0], lb[h - low, s2, b, 1], lb[h - low, s2, b, 2], None)
                for b in range(C)
            ]
            every[rank(h, s2, c)] = guide(cond, uncond)
            for dc in range(1, C):
                send_core(h, s2, dc, every.at[rank(h, s2, c)]).start()

    @pl.loop(0, shared(c))
    def _(h):
        for i, ds, dc in others:
            s2, b = at(ds, dc)
            recv(kv.at[h, b, :, token_rows(rows, s2), :], kv_sem.at[h, s2, b])
            each_relay(i, ds, dc, h, lambda copy: copy.start())

    def hand_on(h):
        for ds in range(1, S):
            s2 = lax.rem(s + ds, S)
            ref = every.at[rank(h, s2, c)]
            recv(ref, out_sem.at[rank(h, s2, c)])
            for dc in range(1, C):
                send_core(h, s2, dc, ref).start()

    for lo, hi, reach in ((0, full(c), W_MAX), (full(c), shared(c), 1)):
        @pl.loop(lo, hi)
        def _(h):
            own_kv(h).wait()
            own_q(h).wait()
            for ds, dc in partners:
                s2, b = at(ds, dc)
                if not ds:
                    recv(kv.at[h, b, :, token_rows(rows, s2), :], kv_sem.at[h, s2, b])
                recv(qb.at[h, b, token_rows(0, s2), :], q_sem.at[h, s2, b])
            for side, ok in ((0, down_ok), (1, up_ok)):
                for ds in range(S):
                    s2 = lax.rem(s + ds, S)

                    @pl.when(ok & crosses(side, s2, h, c))
                    def _():
                        for b in range(C):
                            recv(
                                kv.at[h, b, :, token_rows(halo_base(side), s2), :],
                                halo_sem.at[side, h, s2, b],
                            )
            me = rank(h, s, c)
            window = jnp.int32(0)
            for level in range(1, W_MAX + 1):
                window = window + jnp.where(me < many[level], 1, 0)
            for number in range(frames_here):
                here = f * frames_here + number
                own_shot = seg_ref[here]
                pieces = []
                for offset in range(-reach, reach + 1):
                    there = here + offset
                    shot = seg_ref[jnp.clip(there, 0, frames - 1)]
                    allowed = (
                        (there >= 0) & (there < frames)
                        & (shot == own_shot) & (abs(offset) <= window)
                    )
                    pieces.append(
                        jnp.full((1, per_frame), jnp.where(allowed, 0.0, NEG), jnp.float32)
                    )
                bias = jnp.concatenate(pieces, axis=1)
                keys = pl.ds((frames_here + number - reach) * per_frame, len(pieces) * per_frame)
                mine = pl.ds(number * per_frame, per_frame)
                cond, uncond = [
                    attend(qb[h, b, mine, :], kv[h, b, 0, keys, :], kv[h, b, 1, keys, :], bias)
                    for b in range(C)
                ]
                gb[h, mine, :] = guide(cond, uncond)
            for ds in range(1, S):
                send_out(ds, h).start()
            for dc in range(1, C):
                send_core(h, s, dc, gb.at[h, token_rows(0, s), :]).start()
            every[me] = gb[h, token_rows(0, s), :]

            @pl.when(h > 0)
            def _():
                hand_on(h - 1)

    hand_on(shared(c) - 1)

    @pl.loop(0, near)
    def _(h):
        each_partner(h, lambda *k: send_kv(*k).wait_send())
        each_partner(h, lambda *k: send_q(*k).wait_send())
        each_halo(h, lambda copy: copy.wait_send())

    @pl.loop(0, shared(c))
    def _(h):
        for i, ds, dc in others:
            each_relay(i, ds, dc, h, lambda copy: copy.wait_send())

    each_local(lambda copy: copy.wait_send())

    @pl.loop(0, heads)
    def _(h):
        for s2 in range(S):
            for dc in range(1, C):
                r = rank(h, s2, lax.rem(c + dc, C))
                recv(every.at[r], out_sem.at[r])

    half = heads
    for s2 in range(S):
        for i in range(half):
            head = s2 * (C * half) + c * half + i
            out_ref[i, :, s2 * HD : (s2 + 1) * HD] = every[rank_ref[head]]

    @pl.loop(0, shared(c))
    def _(h):
        for ds in range(1, S):
            send_out(ds, h).wait_send()

    @pl.loop(0, heads)
    def _(h):
        for s2 in range(S):
            for dc in range(1, C):
                send_core(h, s2, dc, every.at[rank(h, s2, c)]).wait_send()


def plan_kernel(heads_all, levels, room, win_ref, plan_ref, fits_ref):
    many = [jnp.int32(0)] * (levels + 2)
    for head in range(heads_all):
        for level in range(1, levels + 1):
            many[level] = many[level] + (win_ref[head] >= level).astype(jnp.int32)
    fits = jnp.int32(1)
    for level in range(1, levels + 1):
        plan_ref[2 * heads_all + level - 1] = many[level]
        fits = fits * (many[level] <= room[level - 1]).astype(jnp.int32)
    fits_ref[0] = fits
    place = [many[level + 1] for level in range(levels + 1)]
    for head in range(heads_all):
        slot = place[0]
        for level in range(1, levels + 1):
            slot = jnp.where(win_ref[head] == level, place[level], slot)
        for level in range(levels + 1):
            place[level] = place[level] + (win_ref[head] == level).astype(jnp.int32)
        plan_ref[slot] = head
        plan_ref[heads_all + head] = slot


def fast_kernel(
    dims, x_ref, plan_ref, time_ref, seg_ref, out_ref,
    xq, xk, xv, qs, kw, qv, qr, tb, tr, ts, tsr, oh, ohr, hs, hr, ov, ovr, vs, ws, wr, gs, gr, every,
    la, lr,
    load_sem, q_send, q_recv, f_send, f_recv, t_send, t_recv, k_send, k_recv, s_send, s_recv,
    c_send, c_recv, w_send, w_recv, g_send, g_recv, h_send, h_recv, e_send, e_recv,
    l_send, l_recv,
):
    F, heads_all, W, M, tl = dims
    N = M - W
    L = heads_all - M
    s = lax.axis_index("seq")
    c = lax.axis_index("cfg")
    f = lax.axis_index("frame")
    frames = 2 * F
    dz = 1 - 2 * s
    up_ok, down_ok = f < F - 1, f > 0
    fwd, back = f + dz, f - dz
    fwd_ok = (fwd >= 0) & (fwd < F)
    back_ok = (back >= 0) & (back < F)
    lanes = [slice(128 * j, 128 * (j + 1)) for j in range(tl // 128)]
    k = len(lanes)

    barrier = pltpu.get_barrier_semaphore()
    for axis, other in (("seq", 1 - s), ("cfg", 1 - c)):
        pl.semaphore_signal(barrier, inc=1, device_id={axis: other}, device_id_type=MESH)
    for ok, step in ((up_ok, 1), (down_ok, -1)):
        @pl.when(ok)
        def _():
            pl.semaphore_signal(
                barrier, inc=1, device_id={"frame": f + step}, device_id_type=MESH
            )

    own = (xq, xk, xv)
    for part, ref in enumerate(own):
        @pl.loop(0, heads_all)
        def _(h):
            pltpu.make_async_copy(
                x_ref.at[part, :, pl.ds(pl.multiple_of(h * HD, HD), HD)], ref.at[h],
                load_sem.at[part],
            ).start()

    def loaded(part):
        pltpu.make_async_copy(own[part], own[part], load_sem.at[part]).wait()

    def remote(src, dst, send, arrive, where):
        return pltpu.make_async_remote_copy(
            src_ref=src, dst_ref=dst, send_sem=send, recv_sem=arrive,
            device_id=where, device_id_type=MESH,
        )

    across = {"seq": 1 - s}
    beside = {"cfg": 1 - c}

    def send_q(i):
        return remote(qs.at[i], qv.at[i], q_send.at[i], q_recv.at[i], across)

    def send_fwd(n):
        return remote(qv.at[W + n], qr.at[n], f_send.at[n], f_recv.at[n], {"frame": fwd})

    def send_third(n):
        return (
            remote(tb.at[n], tr.at[n], t_send.at[0, n], t_recv.at[0, n], {"frame": back}),
            remote(ts.at[n], tsr.at[n], t_send.at[1, n], t_recv.at[1, n], {"frame": back}),
        )

    def send_kv(side, i):
        start = 0 if side == 0 else 2 * tl
        return remote(
            kw.at[i, :, pl.ds(tl, tl), :], kw.at[i, :, pl.ds(start, tl), :],
            k_send.at[side, i], k_recv.at[side, i], {"frame": f + 1 if side == 0 else f - 1},
        )

    def send_stats(i):
        return remote(hs.at[i], hr.at[i], s_send.at[i], s_recv.at[i], across)

    def send_near_stats():
        part = pl.ds(W, N)
        return remote(hs.at[part], hr.at[part], s_send.at[W], s_recv.at[W], across)

    def send_part(i):
        return remote(ov.at[i], ovr.at[i], c_send.at[i], c_recv.at[i], beside)

    def send_weight(i):
        return remote(ws.at[i], wr.at[i], w_send.at[i], w_recv.at[i], across)

    def send_guided(i):
        return remote(gs.at[i], gr.at[i], g_send.at[i], g_recv.at[i], across)

    def send_home(i):
        return remote(oh.at[i], ohr.at[i], h_send.at[i], h_recv.at[i], beside)

    def send_final(i):
        return remote(every.at[i], every.at[i], e_send.at[i], e_recv.at[i], beside)

    def send_local(n):
        return remote(la.at[n], lr.at[n], l_send.at[n], l_recv.at[n], beside)

    def mine(i):
        return lax.rem(i, 2) == c

    factor = LOG2E / math.sqrt(HD)
    rows_id = lax.broadcasted_iota(jnp.int32, (128, 128), 0)
    lanes_id = lax.broadcasted_iota(jnp.int32, (128, 128), 1)
    eye = rows_id == lanes_id
    now = jnp.full((1, HD), time_ref[0], jnp.int32).astype(jnp.float32)
    strength = 1.0 + 4.0 * now / 999.0
    coef = jnp.where(c == 0, strength, 1.0 - strength)

    def to_row(column):
        return [
            jnp.sum(jnp.where(eye, column[part], 0.0), axis=0, keepdims=True) for part in lanes
        ]

    def to_column(row):
        return jnp.concatenate(
            [
                jnp.sum(jnp.where(eye, row[j : j + 1], 0.0), axis=1, keepdims=True)
                for j in range(k)
            ],
            axis=0,
        )

    def attend(query, keys, values, bias=None):
        scores = lax.dot_general(
            query, keys, (((1,), (1,)), ((), ())), preferred_element_type=jnp.float32
        )
        if bias is not None:
            scores = scores + bias
        top = jnp.max(scores, axis=1, keepdims=True)
        expd = jnp.exp2((scores - top) * factor)
        total = jnp.sum(expd, axis=1, keepdims=True)
        part = jnp.dot(expd.astype(jnp.bfloat16), values, preferred_element_type=jnp.float32)
        return part / total, top, total

    def keep_stats(ref, i, top, total):
        for j, row in enumerate(to_row(top) + to_row(total)):
            ref[i, j : j + 1, :] = row

    me = 2 * f + s
    visitor = 2 * f + 1 - s
    beyond = me + 2 * dz

    def shot(frame):
        return seg_ref[jnp.clip(frame, 0, frames - 1)]

    same_visit = shot(me) == shot(visitor)
    same_beyond = fwd_ok & (shot(visitor) == shot(beyond))
    same_low = down_ok & (shot(me) == shot(me - 2))
    same_high = up_ok & (shot(me) == shot(me + 2))

    def reach(level, i):
        return i < plan_ref[2 * heads_all + level - 1]

    def piece(allowed):
        return jnp.full((1, tl), jnp.where(allowed, 0.0, NEG), jnp.float32)

    loaded(0)

    @pl.loop(0, M)
    def _(i):
        qs[i] = xq[plan_ref[i]]

    pl.semaphore_wait(
        barrier, 2 + jnp.where(up_ok, 1, 0) + jnp.where(down_ok, 1, 0)
    )

    @pl.loop(W, M)
    def _(i):
        send_q(i).start()

    loaded(1)
    loaded(2)

    @pl.loop(0, W)
    def _(i):
        for part in range(2):
            kw[i, part, pl.ds(tl, tl), :] = own[1 + part][plan_ref[i]]

    first_kv = [jnp.where(s == side, min(DZ_EARLY, W), min(BACK_EARLY, W)) for side in range(2)]

    def spread_kv(early):
        for side, ok in ((0, up_ok), (1, down_ok)):
            @pl.when(ok)
            def _():
                @pl.loop(0 if early else first_kv[side], first_kv[side] if early else W)
                def _(i):
                    send_kv(side, i).start()

    spread_kv(True)

    for ok, start in ((down_ok, 0), (up_ok, 2 * tl)):
        @pl.when(jnp.logical_not(ok))
        def _():
            @pl.loop(0, W)
            def _(i):
                kw[i, :, pl.ds(start, tl), :] = jnp.zeros((2, tl, HD), kw.dtype)

    @pl.when(jnp.logical_not(fwd_ok))
    def _():
        @pl.loop(0, N)
        def _(n):
            tr[n] = jnp.zeros((tl, HD), tr.dtype)
            tsr[n] = jnp.zeros((2 * k, 128), tsr.dtype)

    @pl.loop(W, M)
    def _(i):
        here = plan_ref[i]
        out, top, total = attend(qs[i], xk[here], xv[here])
        oh[i] = out
        keep_stats(hs, i, top, total)

    send_near_stats().start()

    @pl.loop(0, W)
    def _(i):
        send_q(i).start()

    LAG = 2

    @pl.loop(0, max(N + LAG, L))
    def _(n):
        @pl.when(n < N)
        def _():
            i = W + n
            send_q(i).wait_recv()

            @pl.when(fwd_ok)
            def _():
                send_fwd(n).start()

            here = plan_ref[i]
            out, top, total = attend(qv[i], xk[here], xv[here])
            ov[i] = out
            keep_stats(vs, i, top, total)

        @pl.when((n >= LAG) & (n < N + LAG) & back_ok)
        def _():
            m = n - LAG
            send_fwd(m).wait_recv()
            here = plan_ref[W + m]
            out, top, total = attend(qr[m], xk[here], xv[here])
            tb[m] = out.astype(jnp.bfloat16)
            keep_stats(ts, m, top, total)
            for copy in send_third(m):
                copy.start()

        @pl.when(n < L)
        def _():
            here = plan_ref[M + n]
            out, _, _ = attend(xq[here], xk[here], xv[here])
            la[n] = out.astype(jnp.bfloat16)
            send_local(n).start()

    spread_kv(False)

    def weigh(i, home, parts):
        tops = [
            ref[at, 0:k, :] + jnp.full((1, 128), jnp.where(ok, 0.0, NEG), jnp.float32)
            for ref, at, ok in parts
        ]
        tops.append(home[i, 0:k, :])
        high = functools.reduce(jnp.maximum, tops)
        sums = [ref[at, k : 2 * k, :] for ref, at, _ in parts] + [home[i, k : 2 * k, :]]
        mass = [jnp.exp2((top - high) * factor) * total for top, total in zip(tops, sums)]
        whole = sum(mass)
        shares = [part / whole for part in mass]
        ws[i] = shares[-1]
        send_weight(i).start()
        return [to_column(share) * coef for share in shares[:-1]]

    def hand_over(i):
        @pl.when(jnp.logical_not(mine(i)))
        def _():
            send_part(i).start()

    def join(i):
        @pl.when(mine(i))
        def _():
            send_part(i).wait_recv()
            gs[i] = (ov[i] + ovr[i]).astype(jnp.bfloat16)
            send_guided(i).start()

    def weigh_home(i):
        send_weight(i).wait_recv()
        oh[i] = oh[i] * (to_column(wr[i]) * coef)

        @pl.when(jnp.logical_not(mine(i)))
        def _():
            send_home(i).start()

    def finish(i):
        @pl.when(mine(i))
        def _():
            send_home(i).wait_recv()
            send_guided(i).wait_recv()
            every[i] = (gr[i].astype(jnp.float32) + oh[i] + ohr[i]).astype(jnp.bfloat16)
            send_final(i).start()

    send_near_stats().wait_recv()

    @pl.loop(0, N)
    def _(n):
        i = W + n

        @pl.when(fwd_ok)
        def _():
            for copy in send_third(n):
                copy.wait_recv()

        near = reach(1, i)
        first, second = weigh(
            i, hr, [(vs, i, near & same_visit), (tsr, n, near & same_beyond)]
        )
        ov[i] = first * ov[i] + second * tr[n].astype(jnp.float32)
        hand_over(i)

    @pl.loop(0, L)
    def _(n):
        send_local(n).wait_recv()
        here, there = la[n].astype(jnp.float32), lr[n].astype(jnp.float32)
        cond = jnp.where(c == 0, here, there)
        uncond = jnp.where(c == 0, there, here)
        every[M + n] = (uncond + strength * (cond - uncond)).astype(jnp.bfloat16)

    first_keys = pl.multiple_of(tl * (1 - s), tl)
    per = -(-N // W)

    @pl.loop(0, W + DONE_LAG)
    def _(j):
        @pl.when(j < W)
        def _():
            send_q(j).wait_recv()

            @pl.when(down_ok)
            def _():
                send_kv(0, j).wait_recv()

            @pl.when(up_ok)
            def _():
                send_kv(1, j).wait_recv()

            wide = reach(2, j)
            near = reach(1, j)
            bias = jnp.concatenate(
                [piece(wide & same_low), piece(True), piece(wide & same_high)], axis=1
            )
            out, top, total = attend(qs[j], kw[j, 0], kw[j, 1], bias)
            oh[j] = out
            keep_stats(hs, j, top, total)
            send_stats(j).start()
            one = near & same_visit
            two = near & same_beyond
            bias = jnp.concatenate(
                [
                    piece(jnp.where(s == 0, one, two)),
                    piece(jnp.where(s == 0, two, one)),
                ],
                axis=1,
            )
            keys = pl.ds(first_keys, 2 * tl)
            out, top, total = attend(qv[j], kw[j, 0, keys, :], kw[j, 1, keys, :], bias)
            ov[j] = out
            keep_stats(vs, j, top, total)

        @pl.when((j >= HOST_LAG) & (j < W + HOST_LAG))
        def _():
            m = j - HOST_LAG
            send_stats(m).wait_recv()
            (share,) = weigh(m, hr, [(vs, m, reach(1, m) & (same_visit | same_beyond))])
            ov[m] = share * ov[m]
            hand_over(m)

        for part in range(per):
            n = per * j + part

            @pl.when(n < N)
            def _():
                join(W + n)

            late = per * (j - NEAR_HOME_LAG) + part

            @pl.when((late >= 0) & (late < N))
            def _():
                weigh_home(W + late)

        @pl.when((j >= JOIN_LAG) & (j < W + JOIN_LAG))
        def _():
            join(j - JOIN_LAG)

        @pl.when((j >= HOME_LAG) & (j < W + HOME_LAG))
        def _():
            weigh_home(j - HOME_LAG)

        for part in range(per):
            late = per * (j - NEAR_DONE_LAG) + part

            @pl.when((late >= 0) & (late < N))
            def _():
                finish(W + late)

        @pl.when(j >= DONE_LAG)
        def _():
            finish(j - DONE_LAG)

    @pl.loop(0, M)
    def _(i):
        @pl.when(jnp.logical_not(mine(i)))
        def _():
            send_final(i).wait_recv()

    half = heads_all // 4
    for s2 in range(2):
        for i in range(half):
            head = s2 * (2 * half) + c * half + i
            out_ref[i, :, s2 * HD : (s2 + 1) * HD] = every[plan_ref[heads_all + head]]

    @pl.loop(0, M)
    def _(i):
        send_q(i).wait_send()
        send_weight(i).wait_send()

        @pl.when(mine(i))
        def _():
            send_guided(i).wait_send()
            send_final(i).wait_send()

        @pl.when(jnp.logical_not(mine(i)))
        def _():
            send_part(i).wait_send()
            send_home(i).wait_send()

    @pl.loop(0, N)
    def _(n):
        @pl.when(fwd_ok)
        def _():
            send_fwd(n).wait_send()

        @pl.when(back_ok)
        def _():
            for copy in send_third(n):
                copy.wait_send()

    send_near_stats().wait_send()

    @pl.loop(0, W)
    def _(i):
        send_stats(i).wait_send()
        for side, ok in ((0, up_ok), (1, down_ok)):
            @pl.when(ok)
            def _():
                send_kv(side, i).wait_send()

    @pl.loop(0, L)
    def _(n):
        send_local(n).wait_send()


def fast_call(F, heads_all, W, M, tl, number):
    N, L, k = M - W, heads_all - M, tl // 128
    dma = pltpu.SemaphoreType.DMA

    def block(count, dtype=jnp.bfloat16):
        return pltpu.VMEM((count, tl, HD), dtype)

    def small(count, rows):
        return pltpu.VMEM((count, rows, 128), jnp.float32)

    f32 = jnp.float32
    return pl.pallas_call(
        functools.partial(fast_kernel, (F, heads_all, W, M, tl)),
        out_shape=jax.ShapeDtypeStruct((heads_all // 4, tl, 2 * HD), jnp.bfloat16),
        in_specs=[pl.BlockSpec(memory_space=pl.ANY)]
        + [pl.BlockSpec(memory_space=pltpu.SMEM)] * 3,
        out_specs=pl.BlockSpec(memory_space=pltpu.VMEM),
        scratch_shapes=[
            block(heads_all), block(heads_all), block(heads_all),
            block(M), pltpu.VMEM((W, 2, 3 * tl, HD), jnp.bfloat16), block(M),
            block(N), block(N), block(N), small(N, 2 * k), small(N, 2 * k),
            block(M, f32), block(M, f32), small(M, 2 * k), small(M, 2 * k),
            block(M, f32), block(M, f32), small(M, 2 * k), small(M, k), small(M, k),
            block(M), block(M), block(heads_all), block(L), block(L),
            dma((3,)), dma((M,)), dma((M,)), dma((N,)), dma((N,)), dma((2, N)), dma((2, N)),
            dma((2, W)), dma((2, W)), dma((W + 1,)), dma((W + 1,)),
            dma((M,)), dma((M,)), dma((M,)), dma((M,)), dma((M,)), dma((M,)),
            dma((M,)), dma((M,)), dma((M,)), dma((M,)), dma((L,)), dma((L,)),
        ],
        compiler_params=pltpu.CompilerParams(
            collective_id=number, has_side_effects=True, vmem_limit_bytes=56 * 2**20
        ),
        name=f"visiting_attention_{number}",
    )


def body(qkv, timestep, windows, segments):
    S, C, F = (lax.axis_size(axis) for axis in ("seq", "cfg", "frame"))
    x = jnp.transpose(qkv[0], (1, 0, 2))
    tl = x.shape[1]
    heads = x.shape[2] // HD // (S * C)
    frames_here = segments.shape[0] // F
    assert frames_here == W_MAX and heads * S * C * HD == x.shape[2]
    rows = S * tl
    groups = S * C
    n = groups - 1
    dma = pltpu.SemaphoreType.DMA
    heads_all = heads * groups

    def general(x, timestep, windows, segments):
        ordered, _ = pl.pallas_call(
            functools.partial(gather_kernel, heads_all, W_MAX, (heads_all,) * W_MAX),
            out_shape=(
                jax.ShapeDtypeStruct((heads_all, 3, tl, HD), x.dtype),
                jax.ShapeDtypeStruct((1,), jnp.int32),
            ),
            in_specs=[pl.BlockSpec(memory_space=pl.ANY), pl.BlockSpec(memory_space=pltpu.SMEM)],
            out_specs=(
                pl.BlockSpec(memory_space=pltpu.VMEM),
                pl.BlockSpec(memory_space=pltpu.SMEM),
            ),
            scratch_shapes=[dma],
            name="order_heads",
            compiler_params=pltpu.CompilerParams(vmem_limit_bytes=56 * 2**20),
        )(x, windows)
        kept, near = 1, heads
        return pl.pallas_call(
            functools.partial(kernel, (S, C, F, heads, tl, frames_here, heads, heads, 0)),
            out_shape=jax.ShapeDtypeStruct((heads, tl, S * HD), jnp.bfloat16),
            in_specs=[pl.BlockSpec(memory_space=pl.ANY)]
            + [pl.BlockSpec(memory_space=pltpu.SMEM)] * 3,
            out_specs=pl.BlockSpec(memory_space=pltpu.VMEM),
            scratch_shapes=[
                pltpu.VMEM((near, C, 2, 3 * rows, HD), jnp.bfloat16),
                pltpu.VMEM((near, C, rows, HD), jnp.bfloat16),
                pltpu.VMEM((near, rows, HD), jnp.bfloat16),
                pltpu.VMEM((kept, S, C, 3, tl, HD), jnp.bfloat16),
                pltpu.VMEM((heads_all, tl, HD), jnp.bfloat16),
                pltpu.SMEM((heads_all,), jnp.int32),
                dma((near, S, C)),
                dma((near, S, C)),
                dma((2, near, S, C)),
                dma((heads_all,)),
                dma((2, near, n)),
                dma((2, near, C)),
                dma((2, near, n)),
                dma((near, max(S - 1, 1))),
                dma((heads, S, C - 1)),
                dma((kept, S, C)),
                dma((kept, S, C)),
            ],
            compiler_params=pltpu.CompilerParams(
                collective_id=0, has_side_effects=True, vmem_limit_bytes=40 * 2**20
            ),
            name="guided_attention_0",
        )(ordered, timestep, windows, segments)

    if S == C == frames_here == 2 and tl % 128 == 0 and heads_all >= 8:
        wide, near = heads_all // 3, 2 * heads_all // 3
        plan, fits = pl.pallas_call(
            functools.partial(plan_kernel, heads_all, W_MAX, (near, wide)),
            out_shape=(
                jax.ShapeDtypeStruct((2 * heads_all + W_MAX,), jnp.int32),
                jax.ShapeDtypeStruct((1,), jnp.int32),
            ),
            in_specs=[pl.BlockSpec(memory_space=pltpu.SMEM)],
            out_specs=(pl.BlockSpec(memory_space=pltpu.SMEM),) * 2,
            name="plan_heads",
        )(windows)

        def fast(x, plan, timestep, windows, segments):
            return fast_call(F, heads_all, wide, near, tl, 1)(x, plan, timestep, segments)

        def slow(x, plan, timestep, windows, segments):
            return general(x, timestep, windows, segments)

        out = lax.cond(fits[0] > 0, fast, slow, x, plan, timestep, windows, segments)
    else:
        out = general(x, timestep, windows, segments)
    return jnp.transpose(out, (1, 0, 2))


def solution(mesh):
    return jax.shard_map(
        body,
        mesh=mesh,
        in_specs=(P("cfg", ("groups", "frame", "seq"), None, None), P("groups"), P(), P("groups")),
        out_specs=P(("groups", "frame", "seq"), "cfg", None),
        check_vma=False,
    )
```
